32 devices in a mesh: rows: 32 (over z, y, x, core).
Axes of the slice: x: 2, y: 2, z: 4, core: 2. Of those that a mesh axis runs over, the one named last changes fastest.
Arguments:
- tracers_init: float32 [16384, 256], P('rows'), may hold values from -6 to 6
- source: float32 [16384, 256], P('rows'), may hold values from -4 to 4
- explicit_tiles: float32 [128, 8, 128, 128], P('rows'), may hold values from -0.0625 to 0.0625
- implicit_tiles: float32 [128, 8, 128, 128], P('rows'), may hold values from -0.0625 to 0.0625
- explicit_cols: int32 [128, 8], P('rows'), may hold values from 0 to 6, as said below
- implicit_cols: int32 [128, 8], P('rows'), may hold values from 0 to 6, as said below
- send_rows: int32 [256, 48], P('rows'), may hold values from 0 to 511
Outputs:
- tracers: float32 [16384, 256], P('rows')
The draws below stay inside these ranges and needn't reach their ends.
Inputs may be any that keep to these rules, and one draw needn't show every extreme that they name: `explicit_cols`: each entry names one of the 7 blocks of the device's own rows followed by its halo rows. `implicit_cols`: each entry names one of the 7 blocks of the device's own rows followed by its halo rows. `send_rows`: local row numbers of the sending device.
All inputs are finite; a program needn't handle non-finite values.
Results may differ from the reference program's by a relative error of at most 0.0001.
Values sent between devices are 32-bit elements; how exact they have to be, the bound alone decides.
No kernel may reach another device: no remote copies, remote signals or barrier semaphores. Data moves between devices by JAX's collectives and lax.ppermute only.
A program may use at most 64 MiB of HBM per device.

```python
import jax
import jax.numpy as jnp
from jax import lax

P_SIZE = 256
B = 128
K = 8
NEAR = 4
H = 48
STEPS = 3
NB_DEV = 4
TOTAL_BLK = 128
ROWS = 16384
TOTAL_OFF = 256
EXT_BLK = 7
N_ROWS = 32


def column_pattern(key, salt):
    folded = jax.random.fold_in(key, salt)
    halo_blocks = EXT_BLK - NB_DEV
    columns = jax.random.randint(folded, (TOTAL_BLK, K), 0, EXT_BLK)
    within = jnp.arange(TOTAL_BLK, dtype=jnp.int32) % NB_DEV
    halo_pick = NB_DEV + within % halo_blocks
    first = jnp.where(within < 2 * halo_blocks, halo_pick, columns[:, 0])
    columns = columns.at[:, 0].set(first)
    columns = columns.at[:, 1].set(within)
    return columns.astype(jnp.int32)


def draw_explicit_cols(key, part):
    return column_pattern(key, 11)


def draw_implicit_cols(key, part):
    return column_pattern(key, 23)


def set_ends(values, rng, least, largest):
    index_at = [jax.random.randint(jax.random.fold_in(rng, axis), (), 0, length) for axis, length in enumerate(values.shape)]
    widest = values.shape.index(max(values.shape))
    neighbour = index_at[:widest] + [(index_at[widest] + 1) % values.shape[widest]] + index_at[widest + 1:]
    return values.at[tuple(index_at)].set(least).at[tuple(neighbour)].set(largest)


def levels(own_key, shape, cuts, smallest, largest):
    level = 1.0
    for position, blocks in cuts:
        steps = jax.random.uniform(jax.random.fold_in(jax.random.fold_in(own_key, 6), position), (blocks,), jnp.float32, smallest / len(cuts), largest / len(cuts))
        level = level * jnp.repeat(jnp.exp(steps), shape[position] // blocks).reshape((-1,) + (1,) * (len(shape) - 1 - position))
    return level


def bell_draw(rng, extent, width, limit, cuts=(), held_as=jnp.bfloat16):
    entries = width * jax.random.normal(rng, extent, jnp.float32)
    if cuts:
        entries = entries * levels(rng, extent, cuts, -0.22, 0.18)
    return jnp.clip(entries, -limit, limit).astype(held_as)


def setup_inputs(seed: int = 0) -> dict:
    keys = jax.random.split(jax.random.key(seed), 8)
    return {
        "tracers_init": bell_draw(keys[0], (ROWS, P_SIZE), 1.0, 6.0, ((0, 32),), jnp.float32),
        "source": bell_draw(keys[1], (ROWS, P_SIZE), 0.5, 4.0, ((0, 32),), jnp.float32),
        "explicit_tiles": bell_draw(keys[2], (TOTAL_BLK, K, B, B), (8 * K * B) ** -0.5, 0.0625, ((0, 32),), jnp.float32),
        "implicit_tiles": bell_draw(keys[3], (TOTAL_BLK, K, B, B), (8 * K * B) ** -0.5, 0.0625, ((0, 32),), jnp.float32),
        "explicit_cols": draw_explicit_cols(jax.random.fold_in(keys[7], 71), 0),
        "implicit_cols": draw_implicit_cols(jax.random.fold_in(keys[7], 71), 0),
        "send_rows": set_ends(jax.random.randint(keys[6], (TOTAL_OFF, H), 0, NB_DEV * B), jax.random.fold_in(keys[6], 1), 0, (NB_DEV * B) - 1).astype(jnp.int32),
    }


def partner_offset(offset_index):
    return (offset_index // 2 + 1) * (1 if offset_index % 2 == 0 else -1)


def local_apply(tiles, columns, own_rows, halo_rows):
    extended = jnp.concatenate([own_rows, halo_rows], axis=0).reshape(EXT_BLK, B, P_SIZE)
    total = own_rows.reshape(NB_DEV, B, P_SIZE)
    for slot_index in range(K):
        picked = extended[columns[:, slot_index]]
        total = total + jnp.einsum("rij,rjp->rip", tiles[:, slot_index], picked, precision=lax.Precision.HIGHEST)
    return total.reshape(NB_DEV * B, P_SIZE)


def reference(tracers_init, source, explicit_tiles, implicit_tiles, explicit_cols, implicit_cols, send_rows):
    sends = send_rows.reshape(N_ROWS, 2 * NEAR, H)

    def halo_all(state):
        owned = state.reshape(N_ROWS, NB_DEV * B, P_SIZE)
        payloads = jax.vmap(lambda rows_of, lists: rows_of[lists])(owned, sends)
        pieces = [jnp.roll(payloads[:, offset_index], partner_offset(offset_index), axis=0) for offset_index in range(2 * NEAR)]
        return jnp.concatenate(pieces, axis=1)

    def apply(tiles, columns, state):
        halo = halo_all(state)
        owned = state.reshape(N_ROWS, NB_DEV * B, P_SIZE)
        tiles_dev = tiles.reshape(N_ROWS, NB_DEV, K, B, B)
        columns_dev = columns.reshape(N_ROWS, NB_DEV, K)
        result = lax.map(lambda parts: local_apply(parts[0], parts[1], parts[2], parts[3]), (tiles_dev, columns_dev, owned, halo))
        return result.reshape(N_ROWS * NB_DEV * B, P_SIZE)

    tracers = tracers_init
    for repeat in range(STEPS):
        middle = apply(explicit_tiles, explicit_cols, tracers) + source
        tracers = apply(implicit_tiles, implicit_cols, middle)
    return tracers
```

```python
import functools

import jax
import jax.numpy as jnp
from jax import lax
from jax.experimental import pallas as pl
from jax.experimental.pallas import tpu as pltpu
from jax.sharding import PartitionSpec as P


STEPS = 3
GRANT = 12 * 2**20

VMEM = pl.BlockSpec(memory_space=pltpu.VMEM)
SMEM = pl.BlockSpec(memory_space=pltpu.SMEM)
F32, BF16 = jnp.float32, jnp.bfloat16


def call(kernel, outs, in_specs, args, scratch=()):
    return pl.pallas_call(
        kernel,
        out_shape=[jax.ShapeDtypeStruct(shape, dtype) for shape, dtype in outs],
        in_specs=in_specs,
        out_specs=[VMEM] * len(outs),
        scratch_shapes=list(scratch),
        compiler_params=pltpu.CompilerParams(vmem_limit_bytes=GRANT),
    )(*args)


def from_behind(x, axis, by):
    devices = lax.axis_size(axis)
    return lax.ppermute(x, axis, [(i, (i + by) % devices) for i in range(devices)])


def partner_offset(offset_index):
    return (offset_index // 2 + 1) * (1 if offset_index % 2 == 0 else -1)


def split2(x):
    high = x.astype(BF16)
    return high, (x - high.astype(F32)).astype(BF16)


def dot(a, b):
    return jnp.dot(a, b, preferred_element_type=F32)


def product(m_high, m_low, x_high, x_low):
    return dot(m_high, x_high) + (dot(m_high, x_low) + dot(m_low, x_high))


def pick_rows(onehot, x):
    high = x.astype(BF16)
    rest = x - high.astype(F32)
    mid = rest.astype(BF16)
    low = (rest - mid.astype(F32)).astype(BF16)
    return dot(onehot, high) + (dot(onehot, mid) + dot(onehot, low))


def first_payload_kernel(index, state, *pieces):
    for offset_index, piece in enumerate(pieces):
        def row(i, carry, piece=piece, offset_index=offset_index):
            piece[pl.ds(i, 1), :] = state[pl.ds(index[offset_index, i], 1), :]
            return carry

        lax.fori_loop(0, piece.shape[0], row, 0, unroll=16)


def merge_kernel(columns, tiles, rows, own_high, own_low, far_high, far_low, out_high, out_low, total):
    blocks, slots, size, _ = tiles.shape
    total[...] = jnp.zeros_like(total)
    for block in range(blocks):
        for slot in range(slots):
            column = columns[block, slot]
            total[block, column] += tiles[block, slot]
    for block in range(blocks):
        at = slice(block * size, (block + 1) * size)
        for column in range(total.shape[1]):
            high, low = split2(total[block, column])
            to_high, to_low = (own_high, own_low) if column < blocks else (far_high, far_low)
            place = column if column < blocks else column - blocks
            to_high[at, place * size : (place + 1) * size] = high
            to_low[at, place * size : (place + 1) * size] = low
    onehot = onehot_of(rows, far_high.shape[0])
    out_high[...] = dot(onehot, far_high[...]).astype(BF16)
    out_low[...] = dot(onehot, far_low[...]).astype(BF16)


def onehot_of(rows, width):
    lanes = lax.broadcasted_iota(jnp.int32, (rows.shape[0], width), 1)
    return jnp.where(rows[...] == lanes, 1.0, 0.0).astype(BF16)


def join(pieces, high, low):
    size = pieces[0].shape[0]
    for i, piece in enumerate(pieces):
        h, l = split2(piece[...])
        high[i * size : (i + 1) * size, :] = h
        low[i * size : (i + 1) * size, :] = l


def own_kernel(has_source, partners, *refs):
    refs = list(refs)
    rows, own_high, own_low = refs[:3]
    refs = refs[3:]
    source = refs.pop(0) if has_source else None
    state = refs.pop(0)
    if partners:
        far_high, far_low = refs[:2]
        pieces = refs[2 : 2 + partners]
        refs = refs[2 + partners :]
        base, picked, halo_high, halo_low = refs
        join(pieces, halo_high, halo_low)
        now = state[...] + product(far_high[...], far_low[...], halo_high[...], halo_low[...])
    else:
        base, picked = refs
        now = state[...]
    high, low = split2(now)
    total = now + product(own_high[...], own_low[...], high, low)
    if has_source:
        total = total + source[...]
    base[...] = total
    picked[...] = pick_rows(onehot_of(rows, total.shape[0]), total)


def payload_kernel(partners, *refs):
    picked, out_high, out_low = refs[:3]
    pieces = refs[3 : 3 + partners]
    outs = refs[3 + partners : 3 + 2 * partners]
    halo_high, halo_low = refs[3 + 2 * partners :]
    join(pieces, halo_high, halo_low)
    total = picked[...] + product(out_high[...], out_low[...], halo_high[...], halo_low[...])
    size = outs[0].shape[0]
    for i, out in enumerate(outs):
        out[...] = total[i * size : (i + 1) * size]


def last_kernel(partners, *refs):
    base, far_high, far_low = refs[:3]
    pieces = refs[3 : 3 + partners]
    out, halo_high, halo_low = refs[3 + partners :]
    join(pieces, halo_high, halo_low)
    out[...] = base[...] + product(far_high[...], far_low[...], halo_high[...], halo_low[...])


def on_device(
    tracers_init, source, explicit_tiles, implicit_tiles, explicit_cols, implicit_cols, send_rows
):
    local_rows, panels = tracers_init.shape
    blocks, _, size, _ = explicit_tiles.shape
    partners, halo_size = send_rows.shape
    halo_rows = partners * halo_size
    columns = blocks + halo_rows // size
    halo_scratch = [pltpu.VMEM((halo_rows, panels), BF16)] * 2
    rows = send_rows.reshape(halo_rows, 1)

    def merge(tiles, cols):
        return call(
            merge_kernel,
            [((local_rows, local_rows), BF16)] * 2
            + [((local_rows, halo_rows), BF16)] * 2
            + [((halo_rows, halo_rows), BF16)] * 2,
            [SMEM, VMEM, VMEM],
            (cols, tiles, rows),
            [pltpu.VMEM((blocks, columns, size, size), F32)],
        )

    def exchange(pieces):
        arrived = []
        for offset_index, piece in enumerate(pieces):
            arrived.append(from_behind(piece, "rows", partner_offset(offset_index)))
        return arrived

    applies = 2 * STEPS
    for number in range(applies):
        if number == 0:
            pieces = call(
                first_payload_kernel,
                [((halo_size, panels), F32)] * partners,
                [SMEM, VMEM],
                (send_rows, tracers_init),
            )
        else:
            pieces = call(
                functools.partial(payload_kernel, partners),
                [((halo_size, panels), F32)] * partners,
                [VMEM] * (3 + partners),
                (picked, *last_matrix[4:], *arrived),
                halo_scratch,
            )
        fresh = exchange(pieces)
        if number == 0:
            matrices = (merge(explicit_tiles, explicit_cols), merge(implicit_tiles, implicit_cols))
        matrix = matrices[number % 2]
        has_source = number % 2 == 0
        args = (rows, *matrix[:2]) + ((source,) if has_source else ())
        if number == 0:
            args += (tracers_init,)
        else:
            args += (base, *last_matrix[2:4], *arrived)
        base, picked = call(
            functools.partial(own_kernel, has_source, partners if number else 0),
            [((local_rows, panels), F32), ((halo_rows, panels), F32)],
            [VMEM] * len(args),
            args,
            halo_scratch if number else (),
        )
        arrived, last_matrix = fresh, matrix
    return call(
        functools.partial(last_kernel, partners),
        [((local_rows, panels), F32)],
        [VMEM] * (3 + partners),
        (base, *last_matrix[2:4], *arrived),
        halo_scratch,
    )[0]


def solution(mesh):
    return jax.shard_map(
        on_device,
        mesh=mesh,
        in_specs=(
            P("rows", None),
            P("rows", None),
            P("rows", None, None, None),
            P("rows", None, None, None),
            P("rows", None),
            P("rows", None),
            P("rows", None),
        ),
        out_specs=P("rows", None),
        check_vma=False,
    )
```

```python
import functools

import jax
import jax.numpy as jnp
from jax import lax
from jax.experimental import pallas as pl
from jax.experimental.pallas import tpu as pltpu
from jax.sharding import PartitionSpec as P


STEPS = 3
GRANT = 14 * 2**20

VMEM = pl.BlockSpec(memory_space=pltpu.VMEM)
SMEM = pl.BlockSpec(memory_space=pltpu.SMEM)
F32, BF16 = jnp.float32, jnp.bfloat16


def call(kernel, outs, in_specs, args, scratch=()):
    return pl.pallas_call(
        kernel,
        out_shape=[jax.ShapeDtypeStruct(shape, dtype) for shape, dtype in outs],
        in_specs=in_specs,
        out_specs=[VMEM] * len(outs),
        scratch_shapes=list(scratch),
        compiler_params=pltpu.CompilerParams(vmem_limit_bytes=GRANT),
    )(*args)


def partner_offset(offset_index):
    return (offset_index // 2 + 1) * (1 if offset_index % 2 == 0 else -1)


def routes(partners):
    found = {}
    for sender in range(2):
        for offset_index in range(partners):
            to = sender + partner_offset(offset_index)
            found.setdefault(to // 2, []).append((sender, offset_index, to % 2))
    far = sorted((hop for hop in found if hop > 0)) + sorted((hop for hop in found if hop < 0), reverse=True)
    return [(hop, found[hop]) for hop in [0] + far]


def side():
    return lax.rem(lax.axis_index("rows"), 2)


def swap(x):
    devices = lax.axis_size("rows")
    return lax.ppermute(x, "rows", [(i, i ^ 1) for i in range(devices)])


def split2(x):
    high = x.astype(BF16)
    return high, (x - high.astype(F32)).astype(BF16)


def dot(a, b):
    return jnp.dot(a, b, preferred_element_type=F32)


def product(m_high, m_low, x):
    half = x.shape[1] // 2
    big, small = dot(m_high, x), dot(m_low, x)
    return big[:, :half] + (big[:, half:] + (small[:, :half] + small[:, half:]))


def pick_rows(onehot, x):
    half = x.shape[1]
    high = x.astype(BF16)
    rest = x - high.astype(F32)
    mid = rest.astype(BF16)
    low = (rest - mid.astype(F32)).astype(BF16)
    got = dot(onehot, jnp.concatenate([high, mid, low], axis=1))
    return got[:, :half] + (got[:, half : 2 * half] + got[:, 2 * half :])


def fill_onehot(rows, onehot):
    lists, length = rows.shape
    width = onehot.shape[1]
    down = lax.broadcasted_iota(jnp.int32, (length, length), 0)
    along = lax.broadcasted_iota(jnp.int32, (length, length), 1)
    lanes = lax.broadcasted_iota(jnp.int32, (length, width), 1)
    for i in range(lists):
        spread = jnp.broadcast_to(rows[i : i + 1, :], (length, length))
        column = jnp.sum(jnp.where(down == along, spread, 0).astype(F32), axis=1, keepdims=True)
        hit = jnp.broadcast_to(column, (length, width)) == lanes.astype(F32)
        onehot[i * length : (i + 1) * length, :] = jnp.where(hit, 1.0, 0.0).astype(BF16)


def halves_kernel(x, keep, give):
    half = keep.shape[1]

    @pl.when(side() == 0)
    def _():
        keep[...] = x[:, :half]
        give[...] = x[:, half:]

    @pl.when(side() == 1)
    def _():
        keep[...] = x[:, half:]
        give[...] = x[:, :half]


def merge_kernel(columns, tiles, total):
    blocks, slots = tiles.shape[:2]
    total[...] = jnp.zeros_like(total)
    for block in range(blocks):
        for slot in range(slots):
            column = columns[block, slot]
            total[block, column] += tiles[block, slot]


def split_kernel(total, onehot, own_high, own_low, far_high, far_low, out_high, out_low):
    blocks, columns, size, _ = total.shape
    for block in range(blocks):
        at = slice(block * size, (block + 1) * size)
        for column in range(columns):
            high, low = split2(total[block, column])
            to_high, to_low = (own_high, own_low) if column < blocks else (far_high, far_low)
            place = column if column < blocks else column - blocks
            to_high[at, place * size : (place + 1) * size] = high
            to_low[at, place * size : (place + 1) * size] = low
    out_high[...] = dot(onehot[...], far_high[...]).astype(BF16)
    out_low[...] = dot(onehot[...], far_low[...]).astype(BF16)


def deal(route, lists, outs):
    for (_, group), out in zip(route, outs):
        length = out.shape[0] // len(group)
        for i, (sender, offset_index, _) in enumerate(group):
            out[i * length : (i + 1) * length, :] = lists[sender, offset_index * length : (offset_index + 1) * length, :]


def collect(route, arrived, halo):
    for (_, group), piece in zip(route, arrived):
        length = piece.shape[0] // len(group)
        half = piece.shape[1]
        for i, (_, offset_index, receiver) in enumerate(group):
            high, low = split2(piece[i * length : (i + 1) * length, :])
            at = slice(offset_index * length, (offset_index + 1) * length)
            halo[receiver, at, :half] = high
            halo[receiver, at, half:] = low


def first_kernel(route, mine, other, rows_mine, rows_other, *refs):
    outs = refs[: len(route)]
    onehot_mine, onehot_other, lists = refs[len(route) :]
    fill_onehot(rows_mine, onehot_mine)
    fill_onehot(rows_other, onehot_other)
    lists[side()] = pick_rows(onehot_mine[...], mine[...])
    lists[1 - side()] = pick_rows(onehot_other[...], other[...])
    deal(route, lists, outs)


def own_kernel(route, has_source, first, *refs):
    refs = list(refs)

    def take(count):
        taken = refs[:count]
        del refs[:count]
        return taken

    onehots = take(2)
    owns = [take(2), take(2)]
    sources = take(2) if has_source else None
    states = take(2)
    if not first:
        fars = [take(2), take(2)]
        arrived = take(len(route))
    bases, picks = take(2), take(2)
    if not first:
        (halo,) = refs
        collect(route, arrived, halo)
    for role in range(2):
        now = states[role][...]
        if not first:
            slot = side() if role == 0 else 1 - side()
            now = now + product(fars[role][0][...], fars[role][1][...], halo[slot])
        total = now + product(owns[role][0][...], owns[role][1][...], jnp.concatenate(split2(now), axis=1))
        if has_source:
            total = total + sources[role][...]
        bases[role][...] = total
        picks[role][...] = pick_rows(onehots[role][...], total)


def payload_kernel(route, *refs):
    count = len(route)
    picks, outs_of = refs[:2], (refs[2:4], refs[4:6])
    arrived, outs = refs[6 : 6 + count], refs[6 + count : 6 + 2 * count]
    halo, lists = refs[6 + 2 * count :]
    collect(route, arrived, halo)
    for role in range(2):
        slot = side() if role == 0 else 1 - side()
        lists[slot] = picks[role][...] + product(outs_of[role][0][...], outs_of[role][1][...], halo[slot])
    deal(route, lists, outs)


def last_kernel(route, role, base, far_high, far_low, *refs):
    arrived, (out, halo) = refs[: len(route)], refs[len(route) :]
    collect(route, arrived, halo)
    slot = side() if role == 0 else 1 - side()
    out[...] = base[...] + product(far_high[...], far_low[...], halo[slot])


def join_kernel(kept, got, out):
    half = kept.shape[1]

    @pl.when(side() == 0)
    def _():
        out[:, :half] = kept[...]
        out[:, half:] = got[...]

    @pl.when(side() == 1)
    def _():
        out[:, :half] = got[...]
        out[:, half:] = kept[...]


def on_device(
    tracers_init, source, explicit_tiles, implicit_tiles, explicit_cols, implicit_cols, send_rows
):
    devices = lax.axis_size("rows")
    local_rows, panels = tracers_init.shape
    half = panels // 2
    blocks, _, size, _ = explicit_tiles.shape
    partners, length = send_rows.shape
    halo_rows = partners * length
    columns = blocks + halo_rows // size
    route = routes(partners)
    state_half = ((local_rows, half), F32)
    list_half = ((halo_rows, half), F32)
    pieces_out = [((len(group) * length, half), F32) for _, group in route]
    halo_scratch = pltpu.VMEM((2, halo_rows, panels), BF16)
    lists_scratch = pltpu.VMEM((2, halo_rows, half), F32)

    def halves(x):
        return call(halves_kernel, [state_half] * 2, [VMEM], (x,))

    def merge(tiles, cols):
        return call(merge_kernel, [((blocks, columns, size, size), F32)], [SMEM, VMEM], (cols, tiles))[0]

    def split(total, onehot):
        return call(
            split_kernel,
            [((local_rows, local_rows), BF16)] * 2
            + [((local_rows, halo_rows), BF16)] * 2
            + [((halo_rows, halo_rows), BF16)] * 2,
            [VMEM] * 2,
            (total, onehot),
        )

    def exchange(pieces):
        arrived = [pieces[0]]
        for (hop, _), piece in zip(route[1:], pieces[1:]):
            pairs = [(d, (d + 2 * hop) % devices) for d in range(devices)]
            arrived.append(lax.ppermute(piece, "rows", pairs))
        return arrived

    applies = 2 * STEPS
    for number in range(applies):
        if number == 0:
            rows_other = swap(send_rows)
            state, give = halves(tracers_init)
            state_other = swap(give)
            merged_e = merge(explicit_tiles, explicit_cols)
            merged_e_other = swap(merged_e)
            *pieces, onehot, onehot_other = call(
                functools.partial(first_kernel, route),
                pieces_out + [((halo_rows, local_rows), BF16)] * 2,
                [VMEM] * 4,
                (state, state_other, send_rows, rows_other),
                [lists_scratch],
            )
            states = (state, state_other)
        else:
            pieces = call(
                functools.partial(payload_kernel, route),
                pieces_out,
                [VMEM] * (6 + len(route)),
                (*picks, *matrix[0][4:], *matrix[1][4:], *arrived),
                [halo_scratch, lists_scratch],
            )
        fresh = exchange(pieces)
        if number == 0:
            give_s = halves(source)
            sources = (give_s[0], swap(give_s[1]))
            matrix_e = (split(merged_e, onehot), split(merged_e_other, onehot_other))
            merged_i = merge(implicit_tiles, implicit_cols)
            merged_i_other = swap(merged_i)
        if number == 1:
            matrix_i = (split(merged_i, onehot), split(merged_i_other, onehot_other))
        last_matrix = matrix if number else None
        matrix = matrix_i if number % 2 else matrix_e
        has_source = number % 2 == 0
        args = (onehot, onehot_other, *matrix[0][:2], *matrix[1][:2])
        if has_source:
            args += sources
        args += tuple(states)
        if number:
            args += (*last_matrix[0][2:4], *last_matrix[1][2:4], *arrived)
        out = call(
            functools.partial(own_kernel, route, has_source, number == 0),
            [state_half] * 2 + [list_half] * 2,
            [VMEM] * len(args),
            args,
            [halo_scratch] if number else [],
        )
        states, picks = out[:2], out[2:]
        arrived = fresh

    def last(role):
        return call(
            functools.partial(last_kernel, route, role),
            [state_half],
            [VMEM] * (3 + len(route)),
            (states[role], *matrix[role][2:4], *arrived),
            [halo_scratch],
        )[0]

    got = swap(last(1))
    return call(join_kernel, [((local_rows, panels), F32)], [VMEM] * 2, (last(0), got))[0]


def solution(mesh):
    return jax.shard_map(
        on_device,
        mesh=mesh,
        in_specs=(
            P("rows", None),
            P("rows", None),
            P("rows", None, None, None),
            P("rows", None, None, None),
            P("rows", None),
            P("rows", None),
            P("rows", None),
        ),
        out_specs=P("rows", None),
        check_vma=False,
    )
```

```python
import functools

import jax
import jax.numpy as jnp
from jax import lax
from jax.experimental import pallas as pl
from jax.experimental.pallas import tpu as pltpu
from jax.sharding import PartitionSpec as P


STEPS = 3
GRANT = 14 * 2**20
WHOLE_GRANT = 121 * 2**19

VMEM = pl.BlockSpec(memory_space=pltpu.VMEM)
SMEM = pl.BlockSpec(memory_space=pltpu.SMEM)
ANY = pl.BlockSpec(memory_space=pl.ANY)
F32, BF16 = jnp.float32, jnp.bfloat16


def call(kernel, outs, in_specs, args, scratch=(), grant=GRANT, out_specs=None, aliases=None):
    return pl.pallas_call(
        kernel,
        out_shape=[jax.ShapeDtypeStruct(shape, dtype) for shape, dtype in outs],
        in_specs=in_specs,
        out_specs=out_specs or [VMEM] * len(outs),
        scratch_shapes=list(scratch),
        input_output_aliases=aliases or {},
        compiler_params=pltpu.CompilerParams(vmem_limit_bytes=grant),
    )(*args)


def partner_offset(offset_index):
    return (offset_index // 2 + 1) * (1 if offset_index % 2 == 0 else -1)


def routes(partners):
    found = {}
    for sender in range(2):
        for offset_index in range(partners):
            to = sender + partner_offset(offset_index)
            found.setdefault(to // 2, []).append((sender, offset_index, to % 2))
    far = sorted((hop for hop in found if hop > 0)) + sorted((hop for hop in found if hop < 0), reverse=True)
    return [(hop, found[hop]) for hop in [0] + far]


def side():
    return lax.rem(lax.axis_index("rows"), 2)


def swap(x):
    devices = lax.axis_size("rows")
    return lax.ppermute(x, "rows", [(i, i ^ 1) for i in range(devices)])


def split2(x):
    high = x.astype(BF16)
    return high, (x - high.astype(F32)).astype(BF16)


def dot(a, b):
    return jnp.dot(a, b, preferred_element_type=F32)


def product(m, x):
    half = x.shape[1] // 2
    got = dot(m, jnp.concatenate([x, x], axis=0))
    return got[:, :half] + got[:, half:]


def terms(x):
    return jnp.concatenate(split2(x), axis=1)


def pick_rows(onehot, x):
    half = x.shape[1]
    high = x.astype(BF16)
    rest = x - high.astype(F32)
    mid = rest.astype(BF16)
    low = (rest - mid.astype(F32)).astype(BF16)
    got = dot(onehot, jnp.concatenate([high, mid, low], axis=1))
    return got[:, :half] + (got[:, half : 2 * half] + got[:, 2 * half :])


def on_each_side(body):
    for place in range(2):

        @pl.when(side() == place)
        def _(place=place):
            body(place)


def fill_onehot(rows, onehot):
    lists, length = rows.shape
    width = onehot.shape[1]
    down = lax.broadcasted_iota(jnp.int32, (length, length), 0)
    along = lax.broadcasted_iota(jnp.int32, (length, length), 1)
    lanes = lax.broadcasted_iota(jnp.int32, (length, width), 1)
    for i in range(lists):
        spread = jnp.broadcast_to(rows[i : i + 1, :], (length, length))
        column = jnp.sum(jnp.where(down == along, spread, 0).astype(F32), axis=1, keepdims=True)
        hit = jnp.broadcast_to(column, (length, width)) == lanes.astype(F32)
        onehot[i * length : (i + 1) * length, :] = jnp.where(hit, 1.0, 0.0).astype(BF16)


def halves_kernel(x, keep, give):
    half = keep.shape[1]

    def body(place):
        keep[...] = x[:, place * half : (place + 1) * half]
        give[...] = x[:, (1 - place) * half : (2 - place) * half]

    on_each_side(body)


def fetch_merge_kernel(columns_in, tiles_in, total, columns, tiles, done):
    blocks = tiles.shape[0]
    fetch = [pltpu.make_async_copy(columns_in, columns, done.at[blocks])]
    fetch += [pltpu.make_async_copy(tiles_in.at[i], tiles.at[i], done.at[i]) for i in range(blocks)]
    for copy in fetch:
        copy.start()
    total[...] = jnp.zeros_like(total)
    fetch[0].wait()
    for block in range(blocks):
        fetch[1 + block].wait()
        add_blocks(columns, tiles, total, block)


def add_blocks(columns, tiles, total, block):
    for slot in range(tiles.shape[1]):
        column = columns[block, slot]
        total[block, column] += tiles[block, slot]


def merge_kernel(columns, tiles, total):
    total[...] = jnp.zeros_like(total)
    for block in range(tiles.shape[0]):
        add_blocks(columns, tiles, total, block)


def split_kernel(total, onehot, own, far, out):
    blocks, columns, size, _ = total.shape
    for block in range(blocks):
        at = slice(block * size, (block + 1) * size)
        for column in range(columns):
            to = own if column < blocks else far
            place = (column if column < blocks else column - blocks) * size
            low_place = place + to.shape[1] // 2
            to[at, place : place + size], to[at, low_place : low_place + size] = split2(total[block, column])
    out[...] = dot(onehot[...], far[...]).astype(BF16)


def deal(route, sender, rows, outs):
    for (_, group), out in zip(route, outs):
        length = out.shape[0] // len(group)
        for i, (source, offset_index, _) in enumerate(group):
            if source == sender:
                out[i * length : (i + 1) * length, :] = rows[offset_index * length : (offset_index + 1) * length]


def collect(route, receiver, arrived):
    found = {}
    for (_, group), piece in zip(route, arrived):
        length = piece.shape[0] // len(group)
        for i, (_, offset_index, target) in enumerate(group):
            if target == receiver:
                found[offset_index] = terms(piece[i * length : (i + 1) * length, :])
    return jnp.concatenate([found[i] for i in range(len(found))], axis=0)


def first_kernel(route, mine, other, rows_mine, rows_other, *refs):
    outs = refs[: len(route)]
    onehots = refs[len(route) :]
    fill_onehot(rows_mine, onehots[0])
    fill_onehot(rows_other, onehots[1])
    picked = [pick_rows(onehot[...], state[...]) for onehot, state in zip(onehots, (mine, other))]

    def body(place):
        for role in range(2):
            deal(route, role ^ place, picked[role], outs)

    on_each_side(body)


def own_kernel(route, has_source, first, *refs):
    refs = list(refs)

    def take(count):
        taken = refs[:count]
        del refs[:count]
        return taken

    onehots, owns = take(2), take(2)
    sources = take(2) if has_source else None
    states = take(2)
    if not first:
        fars, arrived = take(2), take(len(route))
    bases, picks = take(2), take(2)

    def body(place):
        now = [state[...] for state in states]
        if not first:
            halos = [collect(route, role ^ place, arrived) for role in range(2)]
            now = [now[role] + product(fars[role][...], halos[role]) for role in range(2)]
        total = [now[role] + product(owns[role][...], terms(now[role])) for role in range(2)]
        if has_source:
            total = [total[role] + sources[role][...] for role in range(2)]
        for role in range(2):
            bases[role][...] = total[role]
            got = dot(onehots[role][...], terms(total[role]))
            half = got.shape[1] // 2
            picks[role][...] = got[:, :half] + got[:, half:]

    if first:
        body(0)
    else:
        on_each_side(body)


def payload_kernel(route, *refs):
    count = len(route)
    picks, outs_of = refs[:2], refs[2:4]
    arrived, outs = refs[4 : 4 + count], refs[4 + count :]

    def body(place):
        halos = [collect(route, role ^ place, arrived) for role in range(2)]
        rows = [picks[role][...] + product(outs_of[role][...], halos[role]) for role in range(2)]
        for role in range(2):
            deal(route, role ^ place, rows[role], outs)

    on_each_side(body)


def give_back_kernel(route, base, far, *refs):
    arrived, out = refs[: len(route)], refs[len(route)]

    def body(place):
        out[...] = base[...] + product(far[...], collect(route, 1 - place, arrived))

    on_each_side(body)


def store_half(half, out, place, done):
    width = half.shape[1]
    copy = pltpu.make_async_copy(half, out.at[:, place * width : (place + 1) * width], done)
    copy.start()
    copy.wait()


def keep_kernel(route, base, far, *refs):
    arrived, (out, half, done) = refs[: len(route)], refs[len(route) :]

    def body(place):
        half[...] = base[...] + product(far[...], collect(route, place, arrived))
        store_half(half, out, place, done)

    on_each_side(body)


def join_kernel(got, begun, out, done):
    on_each_side(lambda place: store_half(got, out, 1 - place, done))


def on_device(
    tracers_init, source, explicit_tiles, implicit_tiles, explicit_cols, implicit_cols, send_rows
):
    devices = lax.axis_size("rows")
    local_rows, panels = tracers_init.shape
    half = panels // 2
    blocks, slots, size, _ = explicit_tiles.shape
    partners, length = send_rows.shape
    halo_rows = partners * length
    columns = blocks + halo_rows // size
    route = routes(partners)
    state_half = ((local_rows, half), F32)
    list_half = ((halo_rows, half), F32)
    pieces_out = [((len(group) * length, half), F32) for _, group in route]

    def halves(x):
        return call(halves_kernel, [state_half] * 2, [VMEM], (x,))

    def merge(tiles, cols):
        return call(merge_kernel, [((blocks, columns, size, size), F32)], [SMEM, VMEM], (cols, tiles))[0]

    def split(total, onehot):
        return call(
            split_kernel,
            [((local_rows, 2 * local_rows), BF16), ((local_rows, 2 * halo_rows), BF16), ((halo_rows, 2 * halo_rows), BF16)],
            [VMEM] * 2,
            (total, onehot),
        )

    def exchange(pieces):
        arrived = [pieces[0]]
        for (hop, _), piece in zip(route[1:], pieces[1:]):
            pairs = [(d, (d + 2 * hop) % devices) for d in range(devices)]
            arrived.append(lax.ppermute(piece, "rows", pairs))
        return arrived

    applies = 2 * STEPS
    for number in range(applies):
        if number == 0:
            rows_other = swap(send_rows)
            state, give = halves(tracers_init)
            state_other = swap(give)
            merged_e = call(
                fetch_merge_kernel,
                [((blocks, columns, size, size), F32)],
                [ANY] * 2,
                (explicit_cols, explicit_tiles),
                [
                    pltpu.SMEM((blocks, slots), jnp.int32),
                    pltpu.VMEM((blocks, slots, size, size), F32),
                    pltpu.SemaphoreType.DMA((blocks + 1,)),
                ],
                WHOLE_GRANT,
            )[0]
            merged_e_other = swap(merged_e)
            *pieces, onehot, onehot_other = call(
                functools.partial(first_kernel, route),
                pieces_out + [((halo_rows, local_rows), BF16)] * 2,
                [VMEM] * 4,
                (state, state_other, send_rows, rows_other),
            )
            states = (state, state_other)
        else:
            pieces = call(
                functools.partial(payload_kernel, route),
                pieces_out,
                [VMEM] * (4 + len(route)),
                (*picks, matrix[0][2], matrix[1][2], *arrived),
            )
        fresh = exchange(pieces)
        if number == 0:
            give_s = halves(source)
            sources = (give_s[0], swap(give_s[1]))
            matrix_e = (split(merged_e, onehot), split(merged_e_other, onehot_other))
            merged_i = merge(implicit_tiles, implicit_cols)
            merged_i_other = swap(merged_i)
        if number == 1:
            matrix_i = (split(merged_i, onehot), split(merged_i_other, onehot_other))
        last_matrix = matrix if number else None
        matrix = matrix_i if number % 2 else matrix_e
        has_source = number % 2 == 0
        args = (onehot, onehot_other, matrix[0][0], matrix[1][0])
        if has_source:
            args += sources
        args += tuple(states)
        if number:
            args += (last_matrix[0][1], last_matrix[1][1], *arrived)
        out = call(
            functools.partial(own_kernel, route, has_source, number == 0),
            [state_half] * 2 + [list_half] * 2,
            [VMEM] * len(args),
            args,
        )
        states, picks = out[:2], out[2:]
        arrived = fresh

    whole = [((local_rows, panels), F32)]
    done = pltpu.SemaphoreType.DMA
    got = swap(
        call(
            functools.partial(give_back_kernel, route),
            [state_half],
            [VMEM] * (2 + len(route)),
            (states[1], matrix[1][1], *arrived),
        )[0]
    )
    begun = call(
        functools.partial(keep_kernel, route),
        whole,
        [VMEM] * (2 + len(route)),
        (states[0], matrix[0][1], *arrived),
        [pltpu.VMEM((local_rows, half), F32), done],
        out_specs=[ANY],
    )
    return call(join_kernel, whole, [VMEM, ANY], (got, *begun), [done], out_specs=[ANY], aliases={1: 0})[0]


def solution(mesh):
    return jax.shard_map(
        on_device,
        mesh=mesh,
        in_specs=(
            P("rows", None),
            P("rows", None),
            P("rows", None, None, None),
            P("rows", None, None, None),
            P("rows", None),
            P("rows", None),
            P("rows", None),
        ),
        out_specs=P("rows", None),
        check_vma=False,
    )
```

```python
import functools

import jax
import jax.numpy as jnp
from jax import lax
from jax.experimental import pallas as pl
from jax.experimental.pallas import tpu as pltpu
from jax.sharding import PartitionSpec as P


STEPS = 3
GRANT = 14 * 2**20
WHOLE_GRANT = 121 * 2**19

VMEM = pl.BlockSpec(memory_space=pltpu.VMEM)
SMEM = pl.BlockSpec(memory_space=pltpu.SMEM)
ANY = pl.BlockSpec(memory_space=pl.ANY)
F32, BF16 = jnp.float32, jnp.bfloat16


def call(kernel, outs, in_specs, args, scratch=(), grant=GRANT, out_specs=None, aliases=None):
    return pl.pallas_call(
        kernel,
        out_shape=[jax.ShapeDtypeStruct(shape, dtype) for shape, dtype in outs],
        in_specs=in_specs,
        out_specs=out_specs or [VMEM] * len(outs),
        scratch_shapes=list(scratch),
        input_output_aliases=aliases or {},
        compiler_params=pltpu.CompilerParams(vmem_limit_bytes=grant),
    )(*args)


def partner_offset(offset_index):
    return (offset_index // 2 + 1) * (1 if offset_index % 2 == 0 else -1)


def plan(partners, pairs):
    found = {}
    for sender in range(2):
        for offset_index in range(partners):
            to = sender + partner_offset(offset_index)
            found.setdefault(to // 2, []).append((sender, offset_index, to % 2))
    local = found.pop(0)
    reach = max(found)
    if reach == 2 and pairs % 4 == 0:
        order = ((2, (1, 0, 1, 1)), (1, (0, 1, 0, 1)), (2, (0, 1, 0, 0)), (1, (1, 0, 1, 0)))
    else:
        order = [(hop, (forward,)) for forward in (1, 0) for hop in range(1, reach + 1)]
    return local, [(hop, forward, found[-hop], found[hop]) for hop, forward in order]


def hop_of(hop, forward, pair):
    return hop if forward[pair % len(forward)] else -hop


def by_pair(table):
    if len(set(table)) == 1:
        return table[0]
    pair = lax.rem(lax.axis_index("rows") // 2, len(table))
    value = table[0]
    for i in range(1, len(table)):
        value = jnp.where(pair == i, table[i], value)
    return value


def sent_forward(step):
    return by_pair(step[1])


def came_forward(step):
    hop, forward = step[:2]
    count = len(forward)
    table = [0] * count
    for pair in range(count):
        table[(pair + hop_of(hop, forward, pair)) % count] = forward[pair]
    return by_pair(table)


def blend(backward, forward, is_forward):
    return backward if backward == forward else backward + is_forward * (forward - backward)


def block(index, length):
    if isinstance(index, int):
        return slice(index * length, (index + 1) * length)
    return pl.ds(pl.multiple_of(index * length, 16), length)


def role_slot(role):
    return side() if role == 0 else 1 - side()


def side():
    return lax.rem(lax.axis_index("rows"), 2)


def swap(x):
    devices = lax.axis_size("rows")
    return lax.ppermute(x, "rows", [(i, i ^ 1) for i in range(devices)])


def split2(x):
    high = x.astype(BF16)
    return high, (x - high.astype(F32)).astype(BF16)


def dot(a, b):
    return jnp.dot(a, b, preferred_element_type=F32)


def product(m, x):
    half = x.shape[1] // 2
    got = dot(m, jnp.concatenate([x, x], axis=0))
    return got[:, :half] + got[:, half:]


def terms(x):
    return jnp.concatenate(split2(x), axis=1)


def pick_rows(onehot, x):
    half = x.shape[1]
    high = x.astype(BF16)
    rest = x - high.astype(F32)
    mid = rest.astype(BF16)
    low = (rest - mid.astype(F32)).astype(BF16)
    got = dot(onehot, jnp.concatenate([high, mid, low], axis=1))
    return got[:, :half] + (got[:, half : 2 * half] + got[:, 2 * half :])


def on_each_side(body):
    for place in range(2):

        @pl.when(side() == place)
        def _(place=place):
            body(place)


def fill_onehot(rows, onehot):
    lists, length = rows.shape
    width = onehot.shape[1]
    down = lax.broadcasted_iota(jnp.int32, (length, length), 0)
    along = lax.broadcasted_iota(jnp.int32, (length, length), 1)
    lanes = lax.broadcasted_iota(jnp.int32, (length, width), 1)
    for i in range(lists):
        spread = jnp.broadcast_to(rows[i : i + 1, :], (length, length))
        column = jnp.sum(jnp.where(down == along, spread, 0).astype(F32), axis=1, keepdims=True)
        hit = jnp.broadcast_to(column, (length, width)) == lanes.astype(F32)
        onehot[i * length : (i + 1) * length, :] = jnp.where(hit, 1.0, 0.0).astype(BF16)


def halves_kernel(x, keep, give):
    half = keep.shape[1]

    def body(place):
        keep[...] = x[:, place * half : (place + 1) * half]
        give[...] = x[:, (1 - place) * half : (2 - place) * half]

    on_each_side(body)


def fetch_merge_kernel(columns_in, tiles_in, total, columns, tiles, done):
    blocks = tiles.shape[0]
    fetch = [pltpu.make_async_copy(columns_in, columns, done.at[blocks])]
    fetch += [pltpu.make_async_copy(tiles_in.at[i], tiles.at[i], done.at[i]) for i in range(blocks)]
    for copy in fetch:
        copy.start()
    total[...] = jnp.zeros_like(total)
    fetch[0].wait()
    for block in range(blocks):
        fetch[1 + block].wait()
        add_blocks(columns, tiles, total, block)


def add_blocks(columns, tiles, total, block):
    for slot in range(tiles.shape[1]):
        column = columns[block, slot]
        total[block, column] += tiles[block, slot]


def merge_kernel(columns, tiles, total):
    total[...] = jnp.zeros_like(total)
    for block in range(tiles.shape[0]):
        add_blocks(columns, tiles, total, block)


def split_kernel(total, onehot, own, far, out):
    blocks, columns, size, _ = total.shape
    for block in range(blocks):
        at = slice(block * size, (block + 1) * size)
        for column in range(columns):
            to = own if column < blocks else far
            place = (column if column < blocks else column - blocks) * size
            low_place = place + to.shape[1] // 2
            to[at, place : place + size], to[at, low_place : low_place + size] = split2(total[block, column])
    out[...] = dot(onehot[...], far[...]).astype(BF16)


def deal(steps, lists, outs):
    local, far = steps
    length = outs[0].shape[0] // len(local)
    for i, (sender, index, _) in enumerate(local):
        outs[0][block(i, length), :] = lists[sender, block(index, length), :]
    for step, out in zip(far, outs[1:]):
        is_forward = sent_forward(step)
        for i, (backward, forward) in enumerate(zip(*step[2:])):
            sender = blend(backward[0], forward[0], is_forward)
            index = blend(backward[1], forward[1], is_forward)
            out[block(i, length), :] = lists[sender, block(index, length), :]


def collect(steps, arrived, halo):
    local, far = steps
    length = arrived[0].shape[0] // len(local)
    for i, (_, index, receiver) in enumerate(local):
        halo[receiver, block(index, length), :] = terms(arrived[0][block(i, length), :])
    for step, piece in zip(far, arrived[1:]):
        is_forward = came_forward(step)
        for i, (backward, forward) in enumerate(zip(*step[2:])):
            receiver = blend(backward[2], forward[2], is_forward)
            index = blend(backward[1], forward[1], is_forward)
            halo[receiver, block(index, length), :] = terms(piece[block(i, length), :])


def first_kernel(steps, mine, other, rows_mine, rows_other, *refs):
    *outs, onehot_mine, onehot_other, lists = refs
    for role, (rows, onehot, state) in enumerate(
        ((rows_mine, onehot_mine, mine), (rows_other, onehot_other, other))
    ):
        fill_onehot(rows, onehot)
        lists[role_slot(role)] = pick_rows(onehot[...], state[...])
    deal(steps, lists, outs)


def own_kernel(steps, has_source, first, last, *refs):
    refs = list(refs)

    def take(count):
        taken = refs[:count]
        del refs[:count]
        return taken

    onehots, owns = take(2), take(2)
    sources = take(2) if has_source else None
    states = take(2)
    if not first:
        fars, arrived = take(2), take(1 + len(steps[1]))
    bases = take(2)
    picks = None if last else take(2)
    now = [state[...] for state in states]
    if not first:
        (halo,) = refs
        collect(steps, arrived, halo)
        now = [now[role] + product(fars[role][...], halo[role_slot(role)]) for role in range(2)]
    total = [now[role] + product(owns[role][...], terms(now[role])) for role in range(2)]
    if has_source:
        total = [total[role] + sources[role][...] for role in range(2)]
    for role in range(2):
        bases[role][...] = total[role]
        if not last:
            got = dot(onehots[role][...], terms(total[role]))
            half = got.shape[1] // 2
            picks[role][...] = got[:, :half] + got[:, half:]


def payload_kernel(steps, *refs):
    count = 1 + len(steps[1])
    picks, outs_of = refs[:2], refs[2:4]
    arrived, outs = refs[4 : 4 + count], refs[4 + count : 4 + 2 * count]
    halo, lists = refs[4 + 2 * count :]
    collect(steps, arrived, halo)
    rows = [picks[role][...] + product(outs_of[role][...], halo[role_slot(role)]) for role in range(2)]
    for role in range(2):
        lists[role_slot(role)] = rows[role]
    deal(steps, lists, outs)


def give_back_kernel(steps, base, far, *refs):
    *arrived, out, halo = refs
    collect(steps, arrived, halo)
    out[...] = base[...] + product(far[...], halo[role_slot(1)])


def store_half(half, out, place, done):
    width = half.shape[1]
    copy = pltpu.make_async_copy(half, out.at[:, place * width : (place + 1) * width], done)
    copy.start()
    copy.wait()


def keep_kernel(steps, base, far, *refs):
    *arrived, out, half, done, halo = refs
    collect(steps, arrived, halo)
    half[...] = base[...] + product(far[...], halo[role_slot(0)])
    on_each_side(lambda place: store_half(half, out, place, done))


def join_kernel(got, begun, out, done):
    on_each_side(lambda place: store_half(got, out, 1 - place, done))


def on_device(
    tracers_init, source, explicit_tiles, implicit_tiles, explicit_cols, implicit_cols, send_rows
):
    devices = lax.axis_size("rows")
    local_rows, panels = tracers_init.shape
    half = panels // 2
    blocks, slots, size, _ = explicit_tiles.shape
    partners, length = send_rows.shape
    halo_rows = partners * length
    columns = blocks + halo_rows // size
    local, far = steps = plan(partners, devices // 2)
    count = 1 + len(far)
    state_half = ((local_rows, half), F32)
    list_half = ((halo_rows, half), F32)
    pieces_out = [((len(lists) * length, half), F32) for lists in (local, *(step[2] for step in far))]
    halo_scratch = pltpu.VMEM((2, halo_rows, panels), BF16)
    lists_scratch = pltpu.VMEM((2, halo_rows, half), F32)

    def halves(x):
        return call(halves_kernel, [state_half] * 2, [VMEM], (x,))

    def merge(tiles, cols):
        return call(merge_kernel, [((blocks, columns, size, size), F32)], [SMEM, VMEM], (cols, tiles))[0]

    def split(total, onehot):
        return call(
            split_kernel,
            [((local_rows, 2 * local_rows), BF16), ((local_rows, 2 * halo_rows), BF16), ((halo_rows, 2 * halo_rows), BF16)],
            [VMEM] * 2,
            (total, onehot),
        )

    def exchange(pieces):
        arrived = [pieces[0]]
        for (hop, forward, _, _), piece in zip(far, pieces[1:]):
            pairs = [(d, (d + 2 * hop_of(hop, forward, d // 2)) % devices) for d in range(devices)]
            arrived.append(lax.ppermute(piece, "rows", pairs))
        return arrived

    applies = 2 * STEPS
    for number in range(applies):
        if number == 0:
            rows_other = swap(send_rows)
            state, give = halves(tracers_init)
            state_other = swap(give)
            merged_e = call(
                fetch_merge_kernel,
                [((blocks, columns, size, size), F32)],
                [ANY] * 2,
                (explicit_cols, explicit_tiles),
                [
                    pltpu.SMEM((blocks, slots), jnp.int32),
                    pltpu.VMEM((blocks, slots, size, size), F32),
                    pltpu.SemaphoreType.DMA((blocks + 1,)),
                ],
                WHOLE_GRANT,
            )[0]
            merged_e_other = swap(merged_e)
            *pieces, onehot, onehot_other = call(
                functools.partial(first_kernel, steps),
                pieces_out + [((halo_rows, local_rows), BF16)] * 2,
                [VMEM] * 4,
                (state, state_other, send_rows, rows_other),
                [lists_scratch],
            )
            states = (state, state_other)
            later_tiles, later_cols = implicit_tiles, implicit_cols
        else:
            pieces = call(
                functools.partial(payload_kernel, steps),
                pieces_out,
                [VMEM] * (4 + count),
                (*picks, matrix[0][2], matrix[1][2], *arrived),
                [halo_scratch, lists_scratch],
            )
        fresh = exchange(pieces)
        if number == 0:
            give_s = halves(source)
            sources = (give_s[0], swap(give_s[1]))
            matrix_e = (split(merged_e, onehot), split(merged_e_other, onehot_other))
            merged_i = merge(later_tiles, later_cols)
            merged_i_other = swap(merged_i)
        if number == 1:
            matrix_i = (split(merged_i, onehot), split(merged_i_other, onehot_other))
        last_matrix = matrix if number else None
        matrix = matrix_i if number % 2 else matrix_e
        has_source = number % 2 == 0
        args = (onehot, onehot_other, matrix[0][0], matrix[1][0])
        if has_source:
            args += sources
        args += tuple(states)
        if number:
            args += (last_matrix[0][1], last_matrix[1][1], *arrived)
        out = call(
            functools.partial(own_kernel, steps, has_source, number == 0, number == applies - 1),
            [state_half] * 2 + [list_half] * (2 if number < applies - 1 else 0),
            [VMEM] * len(args),
            args,
            [halo_scratch] if number else [],
        )
        states, picks = out[:2], out[2:]
        arrived = fresh

    whole = [((local_rows, panels), F32)]
    done = pltpu.SemaphoreType.DMA
    got = swap(
        call(
            functools.partial(give_back_kernel, steps),
            [state_half],
            [VMEM] * (2 + count),
            (states[1], matrix[1][1], *arrived),
            [halo_scratch],
        )[0]
    )
    begun = call(
        functools.partial(keep_kernel, steps),
        whole,
        [VMEM] * (2 + count),
        (states[0], matrix[0][1], *arrived),
        [pltpu.VMEM((local_rows, half), F32), done, halo_scratch],
        out_specs=[ANY],
    )
    return call(join_kernel, whole, [VMEM, ANY], (got, *begun), [done], out_specs=[ANY], aliases={1: 0})[0]


def solution(mesh):
    return jax.shard_map(
        on_device,
        mesh=mesh,
        in_specs=(
            P("rows", None),
            P("rows", None),
            P("rows", None, None, None),
            P("rows", None, None, None),
            P("rows", None),
            P("rows", None),
            P("rows", None),
        ),
        out_specs=P("rows", None),
        check_vma=False,
    )
```

```python
import functools

import jax
import jax.numpy as jnp
from jax import lax
from jax.experimental import pallas as pl
from jax.experimental.pallas import tpu as pltpu
from jax.sharding import PartitionSpec as P


STEPS = 3
GRANT = 14 * 2**20
COST = 2 * 10**9

VMEM = pl.BlockSpec(memory_space=pltpu.VMEM)
SMEM = pl.BlockSpec(memory_space=pltpu.SMEM)
ANY = pl.BlockSpec(memory_space=pl.ANY)
F32, BF16 = jnp.float32, jnp.bfloat16


def call(kernel, outs, in_specs, args, scratch=(), grant=GRANT, out_specs=None, aliases=None, cost=COST):
    return pl.pallas_call(
        kernel,
        out_shape=[jax.ShapeDtypeStruct(shape, dtype) for shape, dtype in outs],
        in_specs=in_specs,
        out_specs=out_specs or [VMEM] * len(outs),
        scratch_shapes=list(scratch),
        input_output_aliases=aliases or {},
        cost_estimate=pl.CostEstimate(flops=cost, bytes_accessed=0, transcendentals=0),
        compiler_params=pltpu.CompilerParams(vmem_limit_bytes=grant),
    )(*args)


def partner_offset(offset_index):
    return (offset_index // 2 + 1) * (1 if offset_index % 2 == 0 else -1)


def plan(partners, pairs):
    found = {}
    for sender in range(2):
        for offset_index in range(partners):
            to = sender + partner_offset(offset_index)
            found.setdefault(to // 2, []).append((sender, offset_index, to % 2))
    local = found.pop(0)
    reach = max(found)
    if reach == 2 and pairs % 4 == 0:
        order = ((2, (1, 0, 1, 1)), (1, (0, 1, 0, 1)), (2, (0, 1, 0, 0)), (1, (1, 0, 1, 0)))
    else:
        order = [(hop, (forward,)) for forward in (1, 0) for hop in range(1, reach + 1)]
    return local, [(hop, forward, found[-hop], found[hop]) for hop, forward in order]


def hop_of(hop, forward, pair):
    return hop if forward[pair % len(forward)] else -hop


def by_pair(table):
    if len(set(table)) == 1:
        return table[0]
    pair = lax.rem(lax.axis_index("rows") // 2, len(table))
    value = table[0]
    for i in range(1, len(table)):
        value = jnp.where(pair == i, table[i], value)
    return value


def sent_forward(step):
    return by_pair(step[1])


def came_forward(step):
    hop, forward = step[:2]
    count = len(forward)
    table = [0] * count
    for pair in range(count):
        table[(pair + hop_of(hop, forward, pair)) % count] = forward[pair]
    return by_pair(table)


def blend(backward, forward, is_forward):
    return backward if backward == forward else backward + is_forward * (forward - backward)


def block(index, length):
    if isinstance(index, int):
        return slice(index * length, (index + 1) * length)
    return pl.ds(pl.multiple_of(index * length, 16), length)


def role_slot(role):
    return side() if role == 0 else 1 - side()


def side():
    return lax.rem(lax.axis_index("rows"), 2)


def swap(x):
    devices = lax.axis_size("rows")
    return lax.ppermute(x, "rows", [(i, i ^ 1) for i in range(devices)])


def split2(x):
    high = x.astype(BF16)
    return high, (x - high.astype(F32)).astype(BF16)


def dot(a, b):
    return jnp.dot(a, b, preferred_element_type=F32)


def product(m, x):
    half = x.shape[1] // 2
    got = dot(m, jnp.concatenate([x, x], axis=0))
    return got[:, :half] + got[:, half:]


def terms(x):
    return jnp.concatenate(split2(x), axis=1)


def pick_rows(onehot, x):
    half = x.shape[1]
    high = x.astype(BF16)
    rest = x - high.astype(F32)
    mid = rest.astype(BF16)
    low = (rest - mid.astype(F32)).astype(BF16)
    got = dot(onehot, jnp.concatenate([high, mid, low], axis=1))
    return got[:, :half] + (got[:, half : 2 * half] + got[:, 2 * half :])


def on_each_side(body):
    for place in range(2):

        @pl.when(side() == place)
        def _(place=place):
            body(place)


def fill_onehot(rows, onehot):
    lists, length = rows.shape
    width = onehot.shape[1]
    down = lax.broadcasted_iota(jnp.int32, (length, length), 0)
    along = lax.broadcasted_iota(jnp.int32, (length, length), 1)
    lanes = lax.broadcasted_iota(jnp.int32, (length, width), 1)
    for i in range(lists):
        spread = jnp.broadcast_to(rows[i : i + 1, :], (length, length))
        column = jnp.sum(jnp.where(down == along, spread, 0).astype(F32), axis=1, keepdims=True)
        hit = jnp.broadcast_to(column, (length, width)) == lanes.astype(F32)
        onehot[i * length : (i + 1) * length, :] = jnp.where(hit, 1.0, 0.0).astype(BF16)


def halves_kernel(x, keep, give):
    half = keep.shape[1]

    def body(place):
        keep[...] = x[:, place * half : (place + 1) * half]
        give[...] = x[:, (1 - place) * half : (2 - place) * half]

    on_each_side(body)


def add_blocks(columns, tiles, total, block):
    for slot in range(tiles.shape[1]):
        column = columns[block, slot]
        total[block, column] += tiles[block, slot]


def merge_kernel(columns, tiles, total):
    total[...] = jnp.zeros_like(total)
    for block in range(tiles.shape[0]):
        add_blocks(columns, tiles, total, block)


def split_kernel(total, onehot, own, far, out):
    blocks, columns, size, _ = total.shape
    for block in range(blocks):
        at = slice(block * size, (block + 1) * size)
        for column in range(columns):
            to = own if column < blocks else far
            place = (column if column < blocks else column - blocks) * size
            low_place = place + to.shape[1] // 2
            to[at, place : place + size], to[at, low_place : low_place + size] = split2(total[block, column])
    out[...] = dot(onehot[...], far[...]).astype(BF16)


def deal(steps, lists, outs):
    local, far = steps
    length = outs[0].shape[0] // len(local)
    for i, (sender, index, _) in enumerate(local):
        outs[0][block(i, length), :] = lists[sender, block(index, length), :]
    for step, out in zip(far, outs[1:]):
        is_forward = sent_forward(step)
        for i, (backward, forward) in enumerate(zip(*step[2:])):
            sender = blend(backward[0], forward[0], is_forward)
            index = blend(backward[1], forward[1], is_forward)
            out[block(i, length), :] = lists[sender, block(index, length), :]


def collect(steps, arrived, halo):
    local, far = steps
    length = arrived[0].shape[0] // len(local)
    for i, (_, index, receiver) in enumerate(local):
        halo[receiver, block(index, length), :] = terms(arrived[0][block(i, length), :])
    for step, piece in zip(far, arrived[1:]):
        is_forward = came_forward(step)
        for i, (backward, forward) in enumerate(zip(*step[2:])):
            receiver = blend(backward[2], forward[2], is_forward)
            index = blend(backward[1], forward[1], is_forward)
            halo[receiver, block(index, length), :] = terms(piece[block(i, length), :])


def first_kernel(steps, mine, other, rows_mine, rows_other, *refs):
    *outs, onehot_mine, onehot_other, lists = refs
    for role, (rows, onehot, state) in enumerate(
        ((rows_mine, onehot_mine, mine), (rows_other, onehot_other, other))
    ):
        fill_onehot(rows, onehot)
        lists[role_slot(role)] = pick_rows(onehot[...], state[...])
    deal(steps, lists, outs)


def own_kernel(steps, has_source, first, last, *refs):
    refs = list(refs)

    def take(count):
        taken = refs[:count]
        del refs[:count]
        return taken

    onehots, owns = take(2), take(2)
    sources = take(2) if has_source else None
    states = take(2)
    if not first:
        fars, arrived = take(2), take(1 + len(steps[1]))
    bases = take(2)
    picks = None if last else take(2)
    now = [state[...] for state in states]
    if not first:
        (halo,) = refs
        collect(steps, arrived, halo)
        now = [now[role] + product(fars[role][...], halo[role_slot(role)]) for role in range(2)]
    total = [now[role] + product(owns[role][...], terms(now[role])) for role in range(2)]
    if has_source:
        total = [total[role] + sources[role][...] for role in range(2)]
    for role in range(2):
        bases[role][...] = total[role]
        if not last:
            got = dot(onehots[role][...], terms(total[role]))
            half = got.shape[1] // 2
            picks[role][...] = got[:, :half] + got[:, half:]


def payload_kernel(steps, *refs):
    count = 1 + len(steps[1])
    picks, outs_of = refs[:2], refs[2:4]
    arrived, outs = refs[4 : 4 + count], refs[4 + count : 4 + 2 * count]
    halo, lists = refs[4 + 2 * count :]
    collect(steps, arrived, halo)
    rows = [picks[role][...] + product(outs_of[role][...], halo[role_slot(role)]) for role in range(2)]
    for role in range(2):
        lists[role_slot(role)] = rows[role]
    deal(steps, lists, outs)


def give_back_kernel(steps, base, far, *refs):
    *arrived, out, halo = refs
    collect(steps, arrived, halo)
    out[...] = base[...] + product(far[...], halo[role_slot(1)])


def store_half(half, out, place, done):
    width = half.shape[1]
    copy = pltpu.make_async_copy(half, out.at[:, place * width : (place + 1) * width], done)
    copy.start()
    copy.wait()


def keep_kernel(steps, base, far, *refs):
    *arrived, out, half, done, halo = refs
    collect(steps, arrived, halo)
    half[...] = base[...] + product(far[...], halo[role_slot(0)])
    on_each_side(lambda place: store_half(half, out, place, done))


def join_kernel(got, begun, out, done):
    on_each_side(lambda place: store_half(got, out, 1 - place, done))


def on_device(
    tracers_init, source, explicit_tiles, implicit_tiles, explicit_cols, implicit_cols, send_rows
):
    devices = lax.axis_size("rows")
    local_rows, panels = tracers_init.shape
    half = panels // 2
    blocks, _, size, _ = explicit_tiles.shape
    partners, length = send_rows.shape
    halo_rows = partners * length
    columns = blocks + halo_rows // size
    local, far = steps = plan(partners, devices // 2)
    count = 1 + len(far)
    state_half = ((local_rows, half), F32)
    list_half = ((halo_rows, half), F32)
    pieces_out = [((len(lists) * length, half), F32) for lists in (local, *(step[2] for step in far))]
    halo_scratch = pltpu.VMEM((2, halo_rows, panels), BF16)
    lists_scratch = pltpu.VMEM((2, halo_rows, half), F32)

    def halves(x):
        return call(halves_kernel, [state_half] * 2, [VMEM], (x,))

    def merge(tiles, cols):
        return call(merge_kernel, [((blocks, columns, size, size), F32)], [SMEM, VMEM], (cols, tiles))[0]

    def split(total, onehot):
        return call(
            split_kernel,
            [((local_rows, 2 * local_rows), BF16), ((local_rows, 2 * halo_rows), BF16), ((halo_rows, 2 * halo_rows), BF16)],
            [VMEM] * 2,
            (total, onehot),
        )

    def exchange(pieces):
        arrived = [pieces[0]]
        for (hop, forward, _, _), piece in zip(far, pieces[1:]):
            pairs = [(d, (d + 2 * hop_of(hop, forward, d // 2)) % devices) for d in range(devices)]
            arrived.append(lax.ppermute(piece, "rows", pairs))
        return arrived

    applies = 2 * STEPS
    for number in range(applies):
        if number == 0:
            rows_other = swap(send_rows)
            state, give = halves(tracers_init)
            state_other = swap(give)
            merged_e = merge(explicit_tiles, explicit_cols)
            merged_e_other = swap(merged_e)
            *pieces, onehot, onehot_other = call(
                functools.partial(first_kernel, steps),
                pieces_out + [((halo_rows, local_rows), BF16)] * 2,
                [VMEM] * 4,
                (state, state_other, send_rows, rows_other),
                [lists_scratch],
            )
            states = (state, state_other)
            later_tiles, later_cols = implicit_tiles, implicit_cols
        else:
            pieces = call(
                functools.partial(payload_kernel, steps),
                pieces_out,
                [VMEM] * (4 + count),
                (*picks, matrix[0][2], matrix[1][2], *arrived),
                [halo_scratch, lists_scratch],
            )
        fresh = exchange(pieces)
        if number == 0:
            give_s = halves(source)
            sources = (give_s[0], swap(give_s[1]))
            matrix_e = (split(merged_e, onehot), split(merged_e_other, onehot_other))
            merged_i = merge(later_tiles, later_cols)
            merged_i_other = swap(merged_i)
        if number == 1:
            matrix_i = (split(merged_i, onehot), split(merged_i_other, onehot_other))
        last_matrix = matrix if number else None
        matrix = matrix_i if number % 2 else matrix_e
        has_source = number % 2 == 0
        args = (onehot, onehot_other, matrix[0][0], matrix[1][0])
        if has_source:
            args += sources
        args += tuple(states)
        if number:
            args += (last_matrix[0][1], last_matrix[1][1], *arrived)
        out = call(
            functools.partial(own_kernel, steps, has_source, number == 0, number == applies - 1),
            [state_half] * 2 + [list_half] * (2 if number < applies - 1 else 0),
            [VMEM] * len(args),
            args,
            [halo_scratch] if number else [],
        )
        states, picks = out[:2], out[2:]
        arrived = fresh

    whole = [((local_rows, panels), F32)]
    done = pltpu.SemaphoreType.DMA
    got = swap(
        call(
            functools.partial(give_back_kernel, steps),
            [state_half],
            [VMEM] * (2 + count),
            (states[1], matrix[1][1], *arrived),
            [halo_scratch],
        )[0]
    )
    begun = call(
        functools.partial(keep_kernel, steps),
        whole,
        [VMEM] * (2 + count),
        (states[0], matrix[0][1], *arrived),
        [pltpu.VMEM((local_rows, half), F32), done, halo_scratch],
        out_specs=[ANY],
    )
    return call(join_kernel, whole, [VMEM, ANY], (got, *begun), [done], out_specs=[ANY], aliases={1: 0})[0]


def solution(mesh):
    return jax.shard_map(
        on_device,
        mesh=mesh,
        in_specs=(
            P("rows", None),
            P("rows", None),
            P("rows", None, None, None),
            P("rows", None, None, None),
            P("rows", None),
            P("rows", None),
            P("rows", None),
        ),
        out_specs=P("rows", None),
        check_vma=False,
    )
```

```python
import functools

import jax
import jax.numpy as jnp
from jax import lax
from jax.experimental import pallas as pl
from jax.experimental.pallas import tpu as pltpu
from jax.sharding import PartitionSpec as P


STEPS = 3
GRANT = 14 * 2**20
COST = 10**9

VMEM = pl.BlockSpec(memory_space=pltpu.VMEM)
SMEM = pl.BlockSpec(memory_space=pltpu.SMEM)
ANY = pl.BlockSpec(memory_space=pl.ANY)
F32, BF16 = jnp.float32, jnp.bfloat16


def call(kernel, outs, in_specs, args, scratch=(), grant=GRANT, out_specs=None, aliases=None, cost=COST):
    return pl.pallas_call(
        kernel,
        out_shape=[jax.ShapeDtypeStruct(shape, dtype) for shape, dtype in outs],
        in_specs=in_specs,
        out_specs=out_specs or [VMEM] * len(outs),
        scratch_shapes=list(scratch),
        input_output_aliases=aliases or {},
        cost_estimate=pl.CostEstimate(flops=cost, bytes_accessed=0, transcendentals=0),
        compiler_params=pltpu.CompilerParams(vmem_limit_bytes=grant),
    )(*args)


def partner_offset(offset_index):
    return (offset_index // 2 + 1) * (1 if offset_index % 2 == 0 else -1)


def plan(partners, pairs):
    found = {}
    for sender in range(2):
        for offset_index in range(partners):
            to = sender + partner_offset(offset_index)
            found.setdefault(to // 2, []).append((sender, offset_index, to % 2))
    local = found.pop(0)
    reach = max(found)
    if reach == 2 and pairs % 4 == 0:
        order = ((2, (1, 0, 1, 1)), (1, (0, 1, 0, 1)), (2, (0, 1, 0, 0)), (1, (1, 0, 1, 0)))
    else:
        order = [(hop, (forward,)) for forward in (1, 0) for hop in range(1, reach + 1)]
    return local, [(hop, forward, found[-hop], found[hop]) for hop, forward in order]


def hop_of(hop, forward, pair):
    return hop if forward[pair % len(forward)] else -hop


def by_pair(table):
    if len(set(table)) == 1:
        return table[0]
    pair = lax.rem(lax.axis_index("rows") // 2, len(table))
    value = table[0]
    for i in range(1, len(table)):
        value = jnp.where(pair == i, table[i], value)
    return value


def sent_forward(step):
    return by_pair(step[1])


def came_forward(step):
    hop, forward = step[:2]
    count = len(forward)
    table = [0] * count
    for pair in range(count):
        table[(pair + hop_of(hop, forward, pair)) % count] = forward[pair]
    return by_pair(table)


def blend(backward, forward, is_forward):
    return backward if backward == forward else backward + is_forward * (forward - backward)


def block(index, length):
    if isinstance(index, int):
        return slice(index * length, (index + 1) * length)
    return pl.ds(pl.multiple_of(index * length, 16), length)


def role_slot(role):
    return side() if role == 0 else 1 - side()


def side():
    return lax.rem(lax.axis_index("rows"), 2)


def swap(x):
    devices = lax.axis_size("rows")
    return lax.ppermute(x, "rows", [(i, i ^ 1) for i in range(devices)])


def split2(x):
    high = x.astype(BF16)
    return high, (x - high.astype(F32)).astype(BF16)


def dot(a, b):
    return jnp.dot(a, b, preferred_element_type=F32)


def product(m, x):
    half = x.shape[1] // 2
    got = dot(m, jnp.concatenate([x, x], axis=0))
    return got[:, :half] + got[:, half:]


def terms(x):
    return jnp.concatenate(split2(x), axis=1)


def pick_rows(onehot, x):
    half = x.shape[1]
    high = x.astype(BF16)
    rest = x - high.astype(F32)
    mid = rest.astype(BF16)
    low = (rest - mid.astype(F32)).astype(BF16)
    got = dot(onehot, jnp.concatenate([high, mid, low], axis=1))
    return got[:, :half] + (got[:, half : 2 * half] + got[:, 2 * half :])


def on_each_side(body):
    for place in range(2):

        @pl.when(side() == place)
        def _(place=place):
            body(place)


def fill_onehot(rows, onehot):
    lists, length = rows.shape
    width = onehot.shape[1]
    down = lax.broadcasted_iota(jnp.int32, (length, length), 0)
    along = lax.broadcasted_iota(jnp.int32, (length, length), 1)
    lanes = lax.broadcasted_iota(jnp.int32, (length, width), 1)
    for i in range(lists):
        spread = jnp.broadcast_to(rows[i : i + 1, :], (length, length))
        column = jnp.sum(jnp.where(down == along, spread, 0).astype(F32), axis=1, keepdims=True)
        hit = jnp.broadcast_to(column, (length, width)) == lanes.astype(F32)
        onehot[i * length : (i + 1) * length, :] = jnp.where(hit, 1.0, 0.0).astype(BF16)


def halves_kernel(x, keep, give):
    half = keep.shape[1]

    def body(place):
        keep[...] = x[:, place * half : (place + 1) * half]
        give[...] = x[:, (1 - place) * half : (2 - place) * half]

    on_each_side(body)


def add_blocks(columns, tiles, total, block):
    for slot in range(tiles.shape[1]):
        column = columns[block, slot]
        total[block, column] += tiles[block, slot]


def merge_kernel(columns, tiles, total):
    total[...] = jnp.zeros_like(total)
    for block in range(tiles.shape[0]):
        add_blocks(columns, tiles, total, block)


def split_kernel(total, onehot, own, far, out):
    blocks, columns, size, _ = total.shape
    for block in range(blocks):
        at = slice(block * size, (block + 1) * size)
        for column in range(columns):
            to = own if column < blocks else far
            place = (column if column < blocks else column - blocks) * size
            low_place = place + to.shape[1] // 2
            to[at, place : place + size], to[at, low_place : low_place + size] = split2(total[block, column])
    out[...] = dot(onehot[...], far[...]).astype(BF16)


def deal(steps, lists, outs):
    local, far = steps
    length = outs[0].shape[0] // len(local)
    for i, (sender, index, _) in enumerate(local):
        outs[0][block(i, length), :] = lists[sender, block(index, length), :]
    for step, out in zip(far, outs[1:]):
        is_forward = sent_forward(step)
        for i, (backward, forward) in enumerate(zip(*step[2:])):
            sender = blend(backward[0], forward[0], is_forward)
            index = blend(backward[1], forward[1], is_forward)
            out[block(i, length), :] = lists[sender, block(index, length), :]


def collect(steps, arrived, halo):
    local, far = steps
    length = arrived[0].shape[0] // len(local)
    for i, (_, index, receiver) in enumerate(local):
        halo[receiver, block(index, length), :] = terms(arrived[0][block(i, length), :])
    for step, piece in zip(far, arrived[1:]):
        is_forward = came_forward(step)
        for i, (backward, forward) in enumerate(zip(*step[2:])):
            receiver = blend(backward[2], forward[2], is_forward)
            index = blend(backward[1], forward[1], is_forward)
            halo[receiver, block(index, length), :] = terms(piece[block(i, length), :])


def first_kernel(steps, mine, other, rows_mine, rows_other, *refs):
    *outs, onehot_mine, onehot_other, lists = refs
    for role, (rows, onehot, state) in enumerate(
        ((rows_mine, onehot_mine, mine), (rows_other, onehot_other, other))
    ):
        fill_onehot(rows, onehot)
        lists[role_slot(role)] = pick_rows(onehot[...], state[...])
    deal(steps, lists, outs)


def own_kernel(steps, has_source, first, last, *refs):
    refs = list(refs)

    def take(count):
        taken = refs[:count]
        del refs[:count]
        return taken

    onehots, owns = take(2), take(2)
    sources = take(2) if has_source else None
    states = take(2)
    if not first:
        fars, arrived = take(2), take(1 + len(steps[1]))
    bases = take(2)
    picks = None if last else take(2)
    now = [state[...] for state in states]
    if not first:
        (halo,) = refs
        collect(steps, arrived, halo)
        now = [now[role] + product(fars[role][...], halo[role_slot(role)]) for role in range(2)]
    total = [now[role] + product(owns[role][...], terms(now[role])) for role in range(2)]
    if has_source:
        total = [total[role] + sources[role][...] for role in range(2)]
    for role in range(2):
        bases[role][...] = total[role]
        if not last:
            got = dot(onehots[role][...], terms(total[role]))
            half = got.shape[1] // 2
            picks[role][...] = got[:, :half] + got[:, half:]


def payload_kernel(steps, *refs):
    count = 1 + len(steps[1])
    picks, outs_of = refs[:2], refs[2:4]
    arrived, outs = refs[4 : 4 + count], refs[4 + count : 4 + 2 * count]
    halo, lists = refs[4 + 2 * count :]
    collect(steps, arrived, halo)
    rows = [picks[role][...] + product(outs_of[role][...], halo[role_slot(role)]) for role in range(2)]
    for role in range(2):
        lists[role_slot(role)] = rows[role]
    deal(steps, lists, outs)


def give_back_kernel(steps, base, far, *refs):
    *arrived, out, halo = refs
    collect(steps, arrived, halo)
    out[...] = base[...] + product(far[...], halo[role_slot(1)])


def store_half(half, out, place, done):
    width = half.shape[1]
    copy = pltpu.make_async_copy(half, out.at[:, place * width : (place + 1) * width], done)
    copy.start()
    copy.wait()


def keep_kernel(steps, base, far, *refs):
    *arrived, out, half, done, halo = refs
    collect(steps, arrived, halo)
    half[...] = base[...] + product(far[...], halo[role_slot(0)])
    on_each_side(lambda place: store_half(half, out, place, done))


def join_kernel(got, begun, out, done):
    on_each_side(lambda place: store_half(got, out, 1 - place, done))


def on_device(
    tracers_init, source, explicit_tiles, implicit_tiles, explicit_cols, implicit_cols, send_rows
):
    devices = lax.axis_size("rows")
    local_rows, panels = tracers_init.shape
    half = panels // 2
    blocks, _, size, _ = explicit_tiles.shape
    partners, length = send_rows.shape
    halo_rows = partners * length
    columns = blocks + halo_rows // size
    local, far = steps = plan(partners, devices // 2)
    count = 1 + len(far)
    state_half = ((local_rows, half), F32)
    list_half = ((halo_rows, half), F32)
    pieces_out = [((len(lists) * length, half), F32) for lists in (local, *(step[2] for step in far))]
    halo_scratch = pltpu.VMEM((2, halo_rows, panels), BF16)
    lists_scratch = pltpu.VMEM((2, halo_rows, half), F32)

    def halves(x, cost):
        return call(halves_kernel, [state_half] * 2, [VMEM], (x,), cost=cost)

    def merge(tiles, cols):
        return call(merge_kernel, [((blocks, columns, size, size), F32)], [SMEM, VMEM], (cols, tiles))[0]

    def split(total, onehot):
        return call(
            split_kernel,
            [((local_rows, 2 * local_rows), BF16), ((local_rows, 2 * halo_rows), BF16), ((halo_rows, 2 * halo_rows), BF16)],
            [VMEM] * 2,
            (total, onehot),
        )

    def exchange(pieces):
        arrived = [pieces[0]]
        for (hop, forward, _, _), piece in zip(far, pieces[1:]):
            pairs = [(d, (d + 2 * hop_of(hop, forward, d // 2)) % devices) for d in range(devices)]
            arrived.append(lax.ppermute(piece, "rows", pairs))
        return arrived

    applies = 2 * STEPS
    for number in range(applies):
        if number == 0:
            rows_other = swap(send_rows)
            state, give = halves(tracers_init, COST)
            state_other = swap(give)
            merged_e = merge(explicit_tiles, explicit_cols)
            merged_e_other = swap(merged_e)
            *pieces, onehot, onehot_other = call(
                functools.partial(first_kernel, steps),
                pieces_out + [((halo_rows, local_rows), BF16)] * 2,
                [VMEM] * 4,
                (state, state_other, send_rows, rows_other),
                [lists_scratch],
            )
            states = (state, state_other)
            later_tiles, later_cols = implicit_tiles, implicit_cols
        else:
            pieces = call(
                functools.partial(payload_kernel, steps),
                pieces_out,
                [VMEM] * (4 + count),
                (*picks, matrix[0][2], matrix[1][2], *arrived),
                [halo_scratch, lists_scratch],
            )
        fresh = exchange(pieces)
        if number == 0:
            give_s = halves(source, COST // 100)
            sources = (give_s[0], swap(give_s[1]))
            matrix_e = (split(merged_e, onehot), split(merged_e_other, onehot_other))
            merged_i = merge(later_tiles, later_cols)
            merged_i_other = swap(merged_i)
        if number == 1:
            matrix_i = (split(merged_i, onehot), split(merged_i_other, onehot_other))
        last_matrix = matrix if number else None
        matrix = matrix_i if number % 2 else matrix_e
        has_source = number % 2 == 0
        args = (onehot, onehot_other, matrix[0][0], matrix[1][0])
        if has_source:
            args += sources
        args += tuple(states)
        if number:
            args += (last_matrix[0][1], last_matrix[1][1], *arrived)
        out = call(
            functools.partial(own_kernel, steps, has_source, number == 0, number == applies - 1),
            [state_half] * 2 + [list_half] * (2 if number < applies - 1 else 0),
            [VMEM] * len(args),
            args,
            [halo_scratch] if number else [],
        )
        states, picks = out[:2], out[2:]
        arrived = fresh

    whole = [((local_rows, panels), F32)]
    done = pltpu.SemaphoreType.DMA
    got = swap(
        call(
            functools.partial(give_back_kernel, steps),
            [state_half],
            [VMEM] * (2 + count),
            (states[1], matrix[1][1], *arrived),
            [halo_scratch],
        )[0]
    )
    begun = call(
        functools.partial(keep_kernel, steps),
        whole,
        [VMEM] * (2 + count),
        (states[0], matrix[0][1], *arrived),
        [pltpu.VMEM((local_rows, half), F32), done, halo_scratch],
        out_specs=[ANY],
    )
    return call(join_kernel, whole, [VMEM, ANY], (got, *begun), [done], out_specs=[ANY], aliases={1: 0})[0]


def solution(mesh):
    return jax.shard_map(
        on_device,
        mesh=mesh,
        in_specs=(
            P("rows", None),
            P("rows", None),
            P("rows", None, None, None),
            P("rows", None, None, None),
            P("rows", None),
            P("rows", None),
            P("rows", None),
        ),
        out_specs=P("rows", None),
        check_vma=False,
    )
```

```python
import functools

import jax
import jax.numpy as jnp
from jax import lax
from jax.experimental import pallas as pl
from jax.experimental.pallas import tpu as pltpu
from jax.sharding import PartitionSpec as P


STEPS = 3
GRANT = 14 * 2**20
COST = 10**9

VMEM = pl.BlockSpec(memory_space=pltpu.VMEM)
SMEM = pl.BlockSpec(memory_space=pltpu.SMEM)
ANY = pl.BlockSpec(memory_space=pl.ANY)
F32, BF16 = jnp.float32, jnp.bfloat16


def call(kernel, outs, in_specs, args, scratch=(), grant=GRANT, out_specs=None, aliases=None, cost=COST):
    return pl.pallas_call(
        kernel,
        out_shape=[jax.ShapeDtypeStruct(shape, dtype) for shape, dtype in outs],
        in_specs=in_specs,
        out_specs=out_specs or [VMEM] * len(outs),
        scratch_shapes=list(scratch),
        input_output_aliases=aliases or {},
        cost_estimate=pl.CostEstimate(flops=cost, bytes_accessed=0, transcendentals=0),
        compiler_params=pltpu.CompilerParams(vmem_limit_bytes=grant),
    )(*args)


def partner_offset(offset_index):
    return (offset_index // 2 + 1) * (1 if offset_index % 2 == 0 else -1)


def plan(partners, pairs):
    found = {}
    for sender in range(2):
        for offset_index in range(partners):
            to = sender + partner_offset(offset_index)
            found.setdefault(to // 2, []).append((sender, offset_index, to % 2))
    local = found.pop(0)
    reach = max(found)
    if reach == 2 and pairs % 4 == 0:
        order = ((2, (1, 0, 1, 1)), (1, (0, 1, 0, 1)), (2, (0, 1, 0, 0)), (1, (1, 0, 1, 0)))
    else:
        order = [(hop, (forward,)) for forward in (1, 0) for hop in range(1, reach + 1)]
    return local, [(hop, forward, found[-hop], found[hop]) for hop, forward in order]


def hop_of(hop, forward, pair):
    return hop if forward[pair % len(forward)] else -hop


def by_pair(table, pair):
    if len(set(table)) == 1:
        return table[0]
    if pair is not None:
        return table[pair % len(table)]
    pair = lax.rem(lax.axis_index("rows") // 2, len(table))
    value = table[0]
    for i in range(1, len(table)):
        value = jnp.where(pair == i, table[i], value)
    return value


def sent_forward(step, pair):
    return by_pair(step[1], pair)


def came_forward(step, pair):
    hop, forward = step[:2]
    count = len(forward)
    table = [0] * count
    for sender in range(count):
        table[(sender + hop_of(hop, forward, sender)) % count] = forward[sender]
    return by_pair(table, pair)


def on_each_pair(steps, body):
    count = max(len(step[1]) for step in steps[1])
    for pair in range(count):

        @pl.when(lax.rem(lax.axis_index("rows") // 2, count) == pair)
        def _(pair=pair):
            body(pair)


def blend(backward, forward, is_forward):
    return backward if backward == forward else backward + is_forward * (forward - backward)


def block(index, length):
    if isinstance(index, int):
        return slice(index * length, (index + 1) * length)
    return pl.ds(pl.multiple_of(index * length, 16), length)


def role_slot(role):
    return side() if role == 0 else 1 - side()


def side():
    return lax.rem(lax.axis_index("rows"), 2)


def swap(x):
    devices = lax.axis_size("rows")
    return lax.ppermute(x, "rows", [(i, i ^ 1) for i in range(devices)])


def split2(x):
    high = x.astype(BF16)
    return high, (x - high.astype(F32)).astype(BF16)


def dot(a, b):
    return jnp.dot(a, b, preferred_element_type=F32)


def product(m, x):
    half = x.shape[1] // 2
    got = dot(m, jnp.concatenate([x, x], axis=0))
    return got[:, :half] + got[:, half:]


def terms(x):
    return jnp.concatenate(split2(x), axis=1)


def pick_rows(onehot, x):
    half = x.shape[1]
    high = x.astype(BF16)
    rest = x - high.astype(F32)
    mid = rest.astype(BF16)
    low = (rest - mid.astype(F32)).astype(BF16)
    got = dot(onehot, jnp.concatenate([high, mid, low], axis=1))
    return got[:, :half] + (got[:, half : 2 * half] + got[:, 2 * half :])


def on_each_side(body):
    for place in range(2):

        @pl.when(side() == place)
        def _(place=place):
            body(place)


def fill_onehot(rows, onehot):
    lists, length = rows.shape
    width = onehot.shape[1]
    down = lax.broadcasted_iota(jnp.int32, (length, length), 0)
    along = lax.broadcasted_iota(jnp.int32, (length, length), 1)
    lanes = lax.broadcasted_iota(jnp.int32, (length, width), 1)
    for i in range(lists):
        spread = jnp.broadcast_to(rows[i : i + 1, :], (length, length))
        column = jnp.sum(jnp.where(down == along, spread, 0).astype(F32), axis=1, keepdims=True)
        hit = jnp.broadcast_to(column, (length, width)) == lanes.astype(F32)
        onehot[i * length : (i + 1) * length, :] = jnp.where(hit, 1.0, 0.0).astype(BF16)


def halves_kernel(x, keep, give):
    half = keep.shape[1]

    def body(place):
        keep[...] = x[:, place * half : (place + 1) * half]
        give[...] = x[:, (1 - place) * half : (2 - place) * half]

    on_each_side(body)


def add_blocks(columns, tiles, total, block):
    for slot in range(tiles.shape[1]):
        column = columns[block, slot]
        total[block, column] += tiles[block, slot]


def merge_kernel(columns, tiles, total):
    total[...] = jnp.zeros_like(total)
    for block in range(tiles.shape[0]):
        add_blocks(columns, tiles, total, block)


def split_kernel(total, onehot, own, far, out):
    blocks, columns, size, _ = total.shape
    for block in range(blocks):
        at = slice(block * size, (block + 1) * size)
        for column in range(columns):
            to = own if column < blocks else far
            place = (column if column < blocks else column - blocks) * size
            low_place = place + to.shape[1] // 2
            to[at, place : place + size], to[at, low_place : low_place + size] = split2(total[block, column])
    out[...] = dot(onehot[...], far[...]).astype(BF16)


def deal(steps, lists, outs, pair=None):
    local, far = steps
    length = outs[0].shape[0] // len(local)
    for i, (sender, index, _) in enumerate(local):
        outs[0][block(i, length), :] = lists[sender, block(index, length), :]
    for step, out in zip(far, outs[1:]):
        is_forward = sent_forward(step, pair)
        for i, (backward, forward) in enumerate(zip(*step[2:])):
            sender = blend(backward[0], forward[0], is_forward)
            index = blend(backward[1], forward[1], is_forward)
            out[block(i, length), :] = lists[sender, block(index, length), :]


def collect(steps, arrived, halo, pair=None):
    local, far = steps
    length = arrived[0].shape[0] // len(local)
    for i, (_, index, receiver) in enumerate(local):
        halo[receiver, block(index, length), :] = terms(arrived[0][block(i, length), :])
    for step, piece in zip(far, arrived[1:]):
        is_forward = came_forward(step, pair)
        for i, (backward, forward) in enumerate(zip(*step[2:])):
            receiver = blend(backward[2], forward[2], is_forward)
            index = blend(backward[1], forward[1], is_forward)
            halo[receiver, block(index, length), :] = terms(piece[block(i, length), :])


def first_kernel(steps, mine, other, rows_mine, rows_other, *refs):
    *outs, onehot_mine, onehot_other, lists = refs
    for role, (rows, onehot, state) in enumerate(
        ((rows_mine, onehot_mine, mine), (rows_other, onehot_other, other))
    ):
        fill_onehot(rows, onehot)
        lists[role_slot(role)] = pick_rows(onehot[...], state[...])
    on_each_pair(steps, lambda pair: deal(steps, lists, outs, pair))


def own_kernel(steps, has_source, first, last, *refs):
    refs = list(refs)

    def take(count):
        taken = refs[:count]
        del refs[:count]
        return taken

    onehots, owns = take(2), take(2)
    sources = take(2) if has_source else None
    states = take(2)
    if not first:
        fars, arrived = take(2), take(1 + len(steps[1]))
    bases = take(2)
    picks = None if last else take(2)
    now = [state[...] for state in states]
    if not first:
        (halo,) = refs
        collect(steps, arrived, halo)
        now = [now[role] + product(fars[role][...], halo[role_slot(role)]) for role in range(2)]
    total = [now[role] + product(owns[role][...], terms(now[role])) for role in range(2)]
    if has_source:
        total = [total[role] + sources[role][...] for role in range(2)]
    for role in range(2):
        bases[role][...] = total[role]
        if not last:
            got = dot(onehots[role][...], terms(total[role]))
            half = got.shape[1] // 2
            picks[role][...] = got[:, :half] + got[:, half:]


def payload_kernel(steps, *refs):
    count = 1 + len(steps[1])
    picks, outs_of = refs[:2], refs[2:4]
    arrived, outs = refs[4 : 4 + count], refs[4 + count : 4 + 2 * count]
    halo, lists = refs[4 + 2 * count :]

    def body(place, pair):
        collect(steps, arrived, halo, pair)
        for role in range(2):
            slot = role ^ place
            lists[slot] = picks[role][...] + product(outs_of[role][...], halo[slot])
        deal(steps, lists, outs, pair)

    on_each_pair(steps, lambda pair: on_each_side(lambda place: body(place, pair)))


def give_back_kernel(steps, base, far, *refs):
    *arrived, out, halo = refs
    collect(steps, arrived, halo)
    out[...] = base[...] + product(far[...], halo[role_slot(1)])


def store_half(half, out, place, done):
    width = half.shape[1]
    copy = pltpu.make_async_copy(half, out.at[:, place * width : (place + 1) * width], done)
    copy.start()
    copy.wait()


def keep_kernel(steps, base, far, *refs):
    *arrived, out, half, done, halo = refs
    collect(steps, arrived, halo)
    half[...] = base[...] + product(far[...], halo[role_slot(0)])
    on_each_side(lambda place: store_half(half, out, place, done))


def join_kernel(got, begun, out, done):
    on_each_side(lambda place: store_half(got, out, 1 - place, done))


def on_device(
    tracers_init, source, explicit_tiles, implicit_tiles, explicit_cols, implicit_cols, send_rows
):
    devices = lax.axis_size("rows")
    local_rows, panels = tracers_init.shape
    half = panels // 2
    blocks, _, size, _ = explicit_tiles.shape
    partners, length = send_rows.shape
    halo_rows = partners * length
    columns = blocks + halo_rows // size
    local, far = steps = plan(partners, devices // 2)
    count = 1 + len(far)
    state_half = ((local_rows, half), F32)
    list_half = ((halo_rows, half), F32)
    pieces_out = [((len(lists) * length, half), F32) for lists in (local, *(step[2] for step in far))]
    halo_scratch = pltpu.VMEM((2, halo_rows, panels), BF16)
    lists_scratch = pltpu.VMEM((2, halo_rows, half), F32)

    def halves(x, cost):
        return call(halves_kernel, [state_half] * 2, [VMEM], (x,), cost=cost)

    def merge(tiles, cols):
        return call(merge_kernel, [((blocks, columns, size, size), F32)], [SMEM, VMEM], (cols, tiles))[0]

    def split(total, onehot):
        return call(
            split_kernel,
            [((local_rows, 2 * local_rows), BF16), ((local_rows, 2 * halo_rows), BF16), ((halo_rows, 2 * halo_rows), BF16)],
            [VMEM] * 2,
            (total, onehot),
        )

    def exchange(pieces):
        arrived = [pieces[0]]
        for (hop, forward, _, _), piece in zip(far, pieces[1:]):
            pairs = [(d, (d + 2 * hop_of(hop, forward, d // 2)) % devices) for d in range(devices)]
            arrived.append(lax.ppermute(piece, "rows", pairs))
        return arrived

    applies = 2 * STEPS
    for number in range(applies):
        if number == 0:
            rows_other = swap(send_rows)
            state, give = halves(tracers_init, COST)
            state_other = swap(give)
            merged_e = merge(explicit_tiles, explicit_cols)
            merged_e_other = swap(merged_e)
            *pieces, onehot, onehot_other = call(
                functools.partial(first_kernel, steps),
                pieces_out + [((halo_rows, local_rows), BF16)] * 2,
                [VMEM] * 4,
                (state, state_other, send_rows, rows_other),
                [lists_scratch],
            )
            states = (state, state_other)
            later_tiles, later_cols = implicit_tiles, implicit_cols
        else:
            pieces = call(
                functools.partial(payload_kernel, steps),
                pieces_out,
                [VMEM] * (4 + count),
                (*picks, matrix[0][2], matrix[1][2], *arrived),
                [halo_scratch, lists_scratch],
            )
        fresh = exchange(pieces)
        if number == 0:
            give_s = halves(source, COST // 100)
            sources = (give_s[0], swap(give_s[1]))
            matrix_e = (split(merged_e, onehot), split(merged_e_other, onehot_other))
            merged_i = merge(later_tiles, later_cols)
            merged_i_other = swap(merged_i)
        if number == 1:
            matrix_i = (split(merged_i, onehot), split(merged_i_other, onehot_other))
        last_matrix = matrix if number else None
        matrix = matrix_i if number % 2 else matrix_e
        has_source = number % 2 == 0
        args = (onehot, onehot_other, matrix[0][0], matrix[1][0])
        if has_source:
            args += sources
        args += tuple(states)
        if number:
            args += (last_matrix[0][1], last_matrix[1][1], *arrived)
        out = call(
            functools.partial(own_kernel, steps, has_source, number == 0, number == applies - 1),
            [state_half] * 2 + [list_half] * (2 if number < applies - 1 else 0),
            [VMEM] * len(args),
            args,
            [halo_scratch] if number else [],
        )
        states, picks = out[:2], out[2:]
        arrived = fresh

    whole = [((local_rows, panels), F32)]
    done = pltpu.SemaphoreType.DMA
    got = swap(
        call(
            functools.partial(give_back_kernel, steps),
            [state_half],
            [VMEM] * (2 + count),
            (states[1], matrix[1][1], *arrived),
            [halo_scratch],
        )[0]
    )
    begun = call(
        functools.partial(keep_kernel, steps),
        whole,
        [VMEM] * (2 + count),
        (states[0], matrix[0][1], *arrived),
        [pltpu.VMEM((local_rows, half), F32), done, halo_scratch],
        out_specs=[ANY],
    )
    return call(join_kernel, whole, [VMEM, ANY], (got, *begun), [done], out_specs=[ANY], aliases={1: 0})[0]


def solution(mesh):
    return jax.shard_map(
        on_device,
        mesh=mesh,
        in_specs=(
            P("rows", None),
            P("rows", None),
            P("rows", None, None, None),
            P("rows", None, None, None),
            P("rows", None),
            P("rows", None),
            P("rows", None),
        ),
        out_specs=P("rows", None),
        check_vma=False,
    )
```

```python
import functools

import jax
import jax.numpy as jnp
from jax import lax
from jax.experimental import pallas as pl
from jax.experimental.pallas import tpu as pltpu
from jax.sharding import PartitionSpec as P


STEPS = 3
GRANT = 14 * 2**20
COST = 10**9

VMEM = pl.BlockSpec(memory_space=pltpu.VMEM)
SMEM = pl.BlockSpec(memory_space=pltpu.SMEM)
ANY = pl.BlockSpec(memory_space=pl.ANY)
F32, BF16 = jnp.float32, jnp.bfloat16


def call(kernel, outs, in_specs, args, scratch=(), grant=GRANT, out_specs=None, aliases=None, cost=COST):
    return pl.pallas_call(
        kernel,
        out_shape=[jax.ShapeDtypeStruct(shape, dtype) for shape, dtype in outs],
        in_specs=in_specs,
        out_specs=out_specs or [VMEM] * len(outs),
        scratch_shapes=list(scratch),
        input_output_aliases=aliases or {},
        cost_estimate=pl.CostEstimate(flops=cost, bytes_accessed=0, transcendentals=0),
        compiler_params=pltpu.CompilerParams(vmem_limit_bytes=grant),
    )(*args)


def partner_offset(offset_index):
    return (offset_index // 2 + 1) * (1 if offset_index % 2 == 0 else -1)


def plan(partners, pairs):
    found = {}
    for sender in range(2):
        for offset_index in range(partners):
            to = sender + partner_offset(offset_index)
            found.setdefault(to // 2, []).append((sender, offset_index, to % 2))
    local = found.pop(0)
    reach = max(found)
    if reach == 2 and pairs % 4 == 0:
        order = ((2, (1, 0, 1, 1)), (1, (0, 1, 0, 1)), (2, (0, 1, 0, 0)), (1, (1, 0, 1, 0)))
    else:
        order = [(hop, (forward,)) for forward in (1, 0) for hop in range(1, reach + 1)]
    return local, [(hop, forward, found[-hop], found[hop]) for hop, forward in order]


def hop_of(hop, forward, pair):
    return hop if forward[pair % len(forward)] else -hop


def by_pair(table, pair):
    if len(set(table)) == 1:
        return table[0]
    if pair is not None:
        return table[pair % len(table)]
    pair = lax.rem(lax.axis_index("rows") // 2, len(table))
    value = table[0]
    for i in range(1, len(table)):
        value = jnp.where(pair == i, table[i], value)
    return value


def sent_forward(step, pair):
    return by_pair(step[1], pair)


def came_forward(step, pair):
    hop, forward = step[:2]
    count = len(forward)
    table = [0] * count
    for sender in range(count):
        table[(sender + hop_of(hop, forward, sender)) % count] = forward[sender]
    return by_pair(table, pair)


def on_each_pair(steps, body):
    count = max(len(step[1]) for step in steps[1])
    for pair in range(count):

        @pl.when(lax.rem(lax.axis_index("rows") // 2, count) == pair)
        def _(pair=pair):
            body(pair)


def blend(backward, forward, is_forward):
    return backward if backward == forward else backward + is_forward * (forward - backward)


def block(index, length):
    if isinstance(index, int):
        return slice(index * length, (index + 1) * length)
    return pl.ds(pl.multiple_of(index * length, 16), length)


def role_slot(role):
    return side() if role == 0 else 1 - side()


def side():
    return lax.rem(lax.axis_index("rows"), 2)


def swap(x):
    devices = lax.axis_size("rows")
    return lax.ppermute(x, "rows", [(i, i ^ 1) for i in range(devices)])


def split2(x):
    high = x.astype(BF16)
    return high, (x - high.astype(F32)).astype(BF16)


def dot(a, b):
    return jnp.dot(a, b, preferred_element_type=F32)


def product(m, x):
    half = x.shape[1] // 2
    got = dot(m, jnp.concatenate([x, x], axis=0))
    return got[:, :half] + got[:, half:]


def terms(x):
    return jnp.concatenate(split2(x), axis=1)


def pick_rows(onehot, x):
    half = x.shape[1]
    got = dot(onehot, terms(x))
    return got[:, :half] + got[:, half:]


def on_each_side(body):
    for place in range(2):

        @pl.when(side() == place)
        def _(place=place):
            body(place)


def fill_onehot(rows, onehot):
    lists, length = rows.shape
    width = onehot.shape[1]
    down = lax.broadcasted_iota(jnp.int32, (length, length), 0)
    along = lax.broadcasted_iota(jnp.int32, (length, length), 1)
    lanes = lax.broadcasted_iota(jnp.int32, (length, width), 1)
    for i in range(lists):
        spread = jnp.broadcast_to(rows[i : i + 1, :], (length, length))
        column = jnp.sum(jnp.where(down == along, spread, 0).astype(F32), axis=1, keepdims=True)
        hit = jnp.broadcast_to(column, (length, width)) == lanes.astype(F32)
        onehot[i * length : (i + 1) * length, :] = jnp.where(hit, 1.0, 0.0).astype(BF16)


def halves_kernel(x, keep, give):
    half = keep.shape[1]

    def body(place):
        keep[...] = x[:, place * half : (place + 1) * half]
        give[...] = x[:, (1 - place) * half : (2 - place) * half]

    on_each_side(body)


def add_blocks(columns, tiles, total, block):
    for slot in range(tiles.shape[1]):
        column = columns[block, slot]
        total[block, column] += tiles[block, slot]


def merge_kernel(columns, tiles, total):
    total[...] = jnp.zeros_like(total)
    for block in range(tiles.shape[0]):
        add_blocks(columns, tiles, total, block)


def split_kernel(total, onehot, own, far, out):
    blocks, columns, size, _ = total.shape
    for block in range(blocks):
        at = slice(block * size, (block + 1) * size)
        for column in range(columns):
            to = own if column < blocks else far
            place = (column if column < blocks else column - blocks) * size
            low_place = place + to.shape[1] // 2
            to[at, place : place + size], to[at, low_place : low_place + size] = split2(total[block, column])
    out[...] = dot(onehot[...], far[...]).astype(BF16)


def deal(steps, lists, outs, pair=None):
    local, far = steps
    length = outs[0].shape[0] // len(local)
    for i, (sender, index, _) in enumerate(local):
        outs[0][block(i, length), :] = lists[sender, block(index, length), :]
    for step, out in zip(far, outs[1:]):
        is_forward = sent_forward(step, pair)
        for i, (backward, forward) in enumerate(zip(*step[2:])):
            sender = blend(backward[0], forward[0], is_forward)
            index = blend(backward[1], forward[1], is_forward)
            out[block(i, length), :] = lists[sender, block(index, length), :]


def collect(steps, arrived, halo, pair=None):
    local, far = steps
    length = arrived[0].shape[0] // len(local)
    for i, (_, index, receiver) in enumerate(local):
        halo[receiver, block(index, length), :] = terms(arrived[0][block(i, length), :])
    for step, piece in zip(far, arrived[1:]):
        is_forward = came_forward(step, pair)
        for i, (backward, forward) in enumerate(zip(*step[2:])):
            receiver = blend(backward[2], forward[2], is_forward)
            index = blend(backward[1], forward[1], is_forward)
            halo[receiver, block(index, length), :] = terms(piece[block(i, length), :])


def first_kernel(steps, mine, other, rows_mine, rows_other, *refs):
    *outs, onehot_mine, onehot_other, lists = refs
    for role, (rows, onehot, state) in enumerate(
        ((rows_mine, onehot_mine, mine), (rows_other, onehot_other, other))
    ):
        fill_onehot(rows, onehot)
        lists[role_slot(role)] = pick_rows(onehot[...], state[...])
    on_each_pair(steps, lambda pair: deal(steps, lists, outs, pair))


def own_kernel(steps, has_source, first, last, *refs):
    refs = list(refs)

    def take(count):
        taken = refs[:count]
        del refs[:count]
        return taken

    onehots, owns = take(2), take(2)
    sources = take(2) if has_source else None
    states = take(2)
    if not first:
        fars, arrived = take(2), take(1 + len(steps[1]))
    bases = take(2)
    picks = None if last else take(2)
    now = [state[...] for state in states]
    if not first:
        (halo,) = refs
        collect(steps, arrived, halo)
        now = [now[role] + product(fars[role][...], halo[role_slot(role)]) for role in range(2)]
    total = [now[role] + product(owns[role][...], terms(now[role])) for role in range(2)]
    if has_source:
        total = [total[role] + sources[role][...] for role in range(2)]
    for role in range(2):
        bases[role][...] = total[role]
        if not last:
            picks[role][...] = pick_rows(onehots[role][...], total[role])


def payload_kernel(steps, *refs):
    count = 1 + len(steps[1])
    picks, outs_of = refs[:2], refs[2:4]
    arrived, outs = refs[4 : 4 + count], refs[4 + count : 4 + 2 * count]
    halo, lists = refs[4 + 2 * count :]

    def body(place, pair):
        collect(steps, arrived, halo, pair)
        for role in range(2):
            slot = role ^ place
            lists[slot] = picks[role][...] + product(outs_of[role][...], halo[slot])
        deal(steps, lists, outs, pair)

    on_each_pair(steps, lambda pair: on_each_side(lambda place: body(place, pair)))


def give_back_kernel(steps, base, far, *refs):
    *arrived, out, halo = refs
    collect(steps, arrived, halo)
    out[...] = base[...] + product(far[...], halo[role_slot(1)])


def store_half(half, out, place, done):
    width = half.shape[1]
    copy = pltpu.make_async_copy(half, out.at[:, place * width : (place + 1) * width], done)
    copy.start()
    copy.wait()


def keep_kernel(steps, base, far, *refs):
    *arrived, out, half, done, halo = refs
    collect(steps, arrived, halo)
    half[...] = base[...] + product(far[...], halo[role_slot(0)])
    on_each_side(lambda place: store_half(half, out, place, done))


def join_kernel(got, begun, out, done):
    on_each_side(lambda place: store_half(got, out, 1 - place, done))


def on_device(
    tracers_init, source, explicit_tiles, implicit_tiles, explicit_cols, implicit_cols, send_rows
):
    devices = lax.axis_size("rows")
    local_rows, panels = tracers_init.shape
    half = panels // 2
    blocks, _, size, _ = explicit_tiles.shape
    partners, length = send_rows.shape
    halo_rows = partners * length
    columns = blocks + halo_rows // size
    local, far = steps = plan(partners, devices // 2)
    count = 1 + len(far)
    state_half = ((local_rows, half), F32)
    list_half = ((halo_rows, half), F32)
    pieces_out = [((len(lists) * length, half), F32) for lists in (local, *(step[2] for step in far))]
    halo_scratch = pltpu.VMEM((2, halo_rows, panels), BF16)
    lists_scratch = pltpu.VMEM((2, halo_rows, half), F32)

    def halves(x, cost):
        return call(halves_kernel, [state_half] * 2, [VMEM], (x,), cost=cost)

    def merge(tiles, cols):
        return call(merge_kernel, [((blocks, columns, size, size), F32)], [SMEM, VMEM], (cols, tiles))[0]

    def split(total, onehot):
        return call(
            split_kernel,
            [((local_rows, 2 * local_rows), BF16), ((local_rows, 2 * halo_rows), BF16), ((halo_rows, 2 * halo_rows), BF16)],
            [VMEM] * 2,
            (total, onehot),
        )

    def exchange(pieces):
        arrived = [pieces[0]]
        for (hop, forward, _, _), piece in zip(far, pieces[1:]):
            pairs = [(d, (d + 2 * hop_of(hop, forward, d // 2)) % devices) for d in range(devices)]
            arrived.append(lax.ppermute(piece, "rows", pairs))
        return arrived

    applies = 2 * STEPS
    for number in range(applies):
        if number == 0:
            rows_other = swap(send_rows)
            state, give = halves(tracers_init, COST)
            state_other = swap(give)
            merged_e = merge(explicit_tiles, explicit_cols)
            merged_e_other = swap(merged_e)
            *pieces, onehot, onehot_other = call(
                functools.partial(first_kernel, steps),
                pieces_out + [((halo_rows, local_rows), BF16)] * 2,
                [VMEM] * 4,
                (state, state_other, send_rows, rows_other),
                [lists_scratch],
            )
            states = (state, state_other)
            later_tiles, later_cols = implicit_tiles, implicit_cols
        else:
            pieces = call(
                functools.partial(payload_kernel, steps),
                pieces_out,
                [VMEM] * (4 + count),
                (*picks, matrix[0][2], matrix[1][2], *arrived),
                [halo_scratch, lists_scratch],
            )
        fresh = exchange(pieces)
        if number == 0:
            give_s = halves(source, COST // 100)
            sources = (give_s[0], swap(give_s[1]))
            matrix_e = (split(merged_e, onehot), split(merged_e_other, onehot_other))
            merged_i = merge(later_tiles, later_cols)
            merged_i_other = swap(merged_i)
        if number == 1:
            matrix_i = (split(merged_i, onehot), split(merged_i_other, onehot_other))
        last_matrix = matrix if number else None
        matrix = matrix_i if number % 2 else matrix_e
        has_source = number % 2 == 0
        args = (onehot, onehot_other, matrix[0][0], matrix[1][0])
        if has_source:
            args += sources
        args += tuple(states)
        if number:
            args += (last_matrix[0][1], last_matrix[1][1], *arrived)
        out = call(
            functools.partial(own_kernel, steps, has_source, number == 0, number == applies - 1),
            [state_half] * 2 + [list_half] * (2 if number < applies - 1 else 0),
            [VMEM] * len(args),
            args,
            [halo_scratch] if number else [],
        )
        states, picks = out[:2], out[2:]
        arrived = fresh

    whole = [((local_rows, panels), F32)]
    done = pltpu.SemaphoreType.DMA
    got = swap(
        call(
            functools.partial(give_back_kernel, steps),
            [state_half],
            [VMEM] * (2 + count),
            (states[1], matrix[1][1], *arrived),
            [halo_scratch],
        )[0]
    )
    begun = call(
        functools.partial(keep_kernel, steps),
        whole,
        [VMEM] * (2 + count),
        (states[0], matrix[0][1], *arrived),
        [pltpu.VMEM((local_rows, half), F32), done, halo_scratch],
        out_specs=[ANY],
    )
    return call(join_kernel, whole, [VMEM, ANY], (got, *begun), [done], out_specs=[ANY], aliases={1: 0})[0]


def solution(mesh):
    return jax.shard_map(
        on_device,
        mesh=mesh,
        in_specs=(
            P("rows", None),
            P("rows", None),
            P("rows", None, None, None),
            P("rows", None, None, None),
            P("rows", None),
            P("rows", None),
            P("rows", None),
        ),
        out_specs=P("rows", None),
        check_vma=False,
    )
```

```python
import functools

import jax
import jax.numpy as jnp
from jax import lax
from jax.experimental import pallas as pl
from jax.experimental.pallas import tpu as pltpu
from jax.sharding import PartitionSpec as P


STEPS = 3
GRANT = 14 * 2**20
COST = 10**9

VMEM = pl.BlockSpec(memory_space=pltpu.VMEM)
SMEM = pl.BlockSpec(memory_space=pltpu.SMEM)
ANY = pl.BlockSpec(memory_space=pl.ANY)
F32, BF16 = jnp.float32, jnp.bfloat16


def call(kernel, outs, in_specs, args, scratch=(), grant=GRANT, out_specs=None, aliases=None, cost=COST):
    return pl.pallas_call(
        kernel,
        out_shape=[jax.ShapeDtypeStruct(shape, dtype) for shape, dtype in outs],
        in_specs=in_specs,
        out_specs=out_specs or [VMEM] * len(outs),
        scratch_shapes=list(scratch),
        input_output_aliases=aliases or {},
        cost_estimate=pl.CostEstimate(flops=cost, bytes_accessed=0, transcendentals=0),
        compiler_params=pltpu.CompilerParams(vmem_limit_bytes=grant),
    )(*args)


def partner_offset(offset_index):
    return (offset_index // 2 + 1) * (1 if offset_index % 2 == 0 else -1)


def plan(partners, pairs):
    found = {}
    for sender in range(2):
        for offset_index in range(partners):
            to = sender + partner_offset(offset_index)
            found.setdefault(to // 2, []).append((sender, offset_index, to % 2))
    local = found.pop(0)
    reach = max(found)
    if reach == 2 and pairs % 4 == 0:
        order = ((2, (1, 0, 1, 1)), (1, (0, 1, 0, 1)), (2, (0, 1, 0, 0)), (1, (1, 0, 1, 0)))
    else:
        order = [(hop, (forward,)) for forward in (1, 0) for hop in range(1, reach + 1)]
    return local, [(hop, forward, found[-hop], found[hop]) for hop, forward in order]


def hop_of(hop, forward, pair):
    return hop if forward[pair % len(forward)] else -hop


def by_pair(table, pair):
    if len(set(table)) == 1:
        return table[0]
    if pair is not None:
        return table[pair % len(table)]
    pair = lax.rem(lax.axis_index("rows") // 2, len(table))
    value = table[0]
    for i in range(1, len(table)):
        value = jnp.where(pair == i, table[i], value)
    return value


def sent_forward(step, pair):
    return by_pair(step[1], pair)


def came_forward(step, pair):
    hop, forward = step[:2]
    count = len(forward)
    table = [0] * count
    for sender in range(count):
        table[(sender + hop_of(hop, forward, sender)) % count] = forward[sender]
    return by_pair(table, pair)


def on_each_pair(steps, body):
    count = max(len(step[1]) for step in steps[1])
    for pair in range(count):

        @pl.when(lax.rem(lax.axis_index("rows") // 2, count) == pair)
        def _(pair=pair):
            body(pair)


def blend(backward, forward, is_forward):
    return backward if backward == forward else backward + is_forward * (forward - backward)


def block(index, length):
    if isinstance(index, int):
        return slice(index * length, (index + 1) * length)
    return pl.ds(pl.multiple_of(index * length, 16), length)


def role_slot(role):
    return side() if role == 0 else 1 - side()


def side():
    return lax.rem(lax.axis_index("rows"), 2)


def swap(x):
    devices = lax.axis_size("rows")
    return lax.ppermute(x, "rows", [(i, i ^ 1) for i in range(devices)])


def split2(x):
    high = x.astype(BF16)
    return high, (x - high.astype(F32)).astype(BF16)


def dot(a, b):
    return jnp.dot(a, b, preferred_element_type=F32)


def product(m, x):
    half = x.shape[1] // 2
    got = dot(m, jnp.concatenate([x, x], axis=0))
    return got[:, :half] + got[:, half:]


def terms(x):
    return jnp.concatenate(split2(x), axis=1)


def pick_rows(onehot, x):
    half = x.shape[1]
    got = dot(onehot, terms(x))
    return got[:, :half] + got[:, half:]


def on_each_side(body):
    for place in range(2):

        @pl.when(side() == place)
        def _(place=place):
            body(place)


def fill_onehot(rows, onehot):
    lists, length = rows.shape
    width = onehot.shape[1]
    down = lax.broadcasted_iota(jnp.int32, (length, length), 0)
    along = lax.broadcasted_iota(jnp.int32, (length, length), 1)
    lanes = lax.broadcasted_iota(jnp.int32, (length, width), 1)
    for i in range(lists):
        spread = jnp.broadcast_to(rows[i : i + 1, :], (length, length))
        column = jnp.sum(jnp.where(down == along, spread, 0).astype(F32), axis=1, keepdims=True)
        hit = jnp.broadcast_to(column, (length, width)) == lanes.astype(F32)
        onehot[i * length : (i + 1) * length, :] = jnp.where(hit, 1.0, 0.0).astype(BF16)


def halves_kernel(x, keep, give):
    half = keep.shape[1]

    def body(place):
        keep[...] = x[:, place * half : (place + 1) * half]
        give[...] = x[:, (1 - place) * half : (2 - place) * half]

    on_each_side(body)


def add_blocks(columns, tiles, total, block):
    for slot in range(tiles.shape[1]):
        column = columns[block, slot]
        total[block, column] += tiles[block, slot]


def merge_kernel(columns, tiles, total):
    total[...] = jnp.zeros_like(total)
    for block in range(tiles.shape[0]):
        add_blocks(columns, tiles, total, block)


def split_kernel(total, onehot, own, far, out):
    blocks, columns, size, _ = total.shape

    def put(to, first, last):
        for block in range(blocks):
            at = slice(block * size, (block + 1) * size)
            for column in range(first, last):
                place = (column - first) * size
                low_place = place + to.shape[1] // 2
                to[at, place : place + size], to[at, low_place : low_place + size] = split2(total[block, column])

    put(far, blocks, columns)
    out[...] = dot(onehot[...], far[...]).astype(BF16)
    put(own, 0, blocks)


def deal(steps, lists, outs, pair=None):
    local, far = steps
    length = outs[0].shape[0] // len(local)
    for i, (sender, index, _) in enumerate(local):
        outs[0][block(i, length), :] = lists[sender, block(index, length), :]
    for step, out in zip(far, outs[1:]):
        is_forward = sent_forward(step, pair)
        for i, (backward, forward) in enumerate(zip(*step[2:])):
            sender = blend(backward[0], forward[0], is_forward)
            index = blend(backward[1], forward[1], is_forward)
            out[block(i, length), :] = lists[sender, block(index, length), :]


def collect(steps, arrived, halo, pair=None):
    local, far = steps
    length = arrived[0].shape[0] // len(local)
    for i, (_, index, receiver) in enumerate(local):
        halo[receiver, block(index, length), :] = terms(arrived[0][block(i, length), :])
    for step, piece in zip(far, arrived[1:]):
        is_forward = came_forward(step, pair)
        for i, (backward, forward) in enumerate(zip(*step[2:])):
            receiver = blend(backward[2], forward[2], is_forward)
            index = blend(backward[1], forward[1], is_forward)
            halo[receiver, block(index, length), :] = terms(piece[block(i, length), :])


def first_kernel(steps, mine, other, rows_mine, rows_other, *refs):
    *outs, onehot_mine, onehot_other, lists = refs
    for role, (rows, onehot, state) in enumerate(
        ((rows_mine, onehot_mine, mine), (rows_other, onehot_other, other))
    ):
        fill_onehot(rows, onehot)
        lists[role_slot(role)] = pick_rows(onehot[...], state[...])
    on_each_pair(steps, lambda pair: deal(steps, lists, outs, pair))


def own_kernel(steps, has_source, first, last, *refs):
    refs = list(refs)

    def take(count):
        taken = refs[:count]
        del refs[:count]
        return taken

    onehots, owns = take(2), take(2)
    sources = take(2) if has_source else None
    states = take(2)
    if not first:
        fars, arrived = take(2), take(1 + len(steps[1]))
    bases = take(2)
    picks = None if last else take(2)
    now = [state[...] for state in states]
    if not first:
        (halo,) = refs
        collect(steps, arrived, halo)
        now = [now[role] + product(fars[role][...], halo[role_slot(role)]) for role in range(2)]
    total = [now[role] + product(owns[role][...], terms(now[role])) for role in range(2)]
    if has_source:
        total = [total[role] + sources[role][...] for role in range(2)]
    for role in range(2):
        bases[role][...] = total[role]
        if not last:
            picks[role][...] = pick_rows(onehots[role][...], total[role])


def payload_kernel(steps, *refs):
    count = 1 + len(steps[1])
    picks, outs_of = refs[:2], refs[2:4]
    arrived, outs = refs[4 : 4 + count], refs[4 + count : 4 + 2 * count]
    halo, lists = refs[4 + 2 * count :]

    def body(place, pair):
        collect(steps, arrived, halo, pair)
        for role in range(2):
            slot = role ^ place
            lists[slot] = picks[role][...] + product(outs_of[role][...], halo[slot])
        deal(steps, lists, outs, pair)

    on_each_pair(steps, lambda pair: on_each_side(lambda place: body(place, pair)))


def give_back_kernel(steps, base, far, *refs):
    *arrived, out, halo = refs
    collect(steps, arrived, halo)
    out[...] = base[...] + product(far[...], halo[role_slot(1)])


def store_half(half, out, place, done):
    width = half.shape[1]
    copy = pltpu.make_async_copy(half, out.at[:, place * width : (place + 1) * width], done)
    copy.start()
    copy.wait()


def keep_kernel(steps, base, far, *refs):
    *arrived, out, half, done, halo = refs
    collect(steps, arrived, halo)
    half[...] = base[...] + product(far[...], halo[role_slot(0)])
    on_each_side(lambda place: store_half(half, out, place, done))


def join_kernel(got, begun, out, done):
    on_each_side(lambda place: store_half(got, out, 1 - place, done))


def on_device(
    tracers_init, source, explicit_tiles, implicit_tiles, explicit_cols, implicit_cols, send_rows
):
    devices = lax.axis_size("rows")
    local_rows, panels = tracers_init.shape
    half = panels // 2
    blocks, _, size, _ = explicit_tiles.shape
    partners, length = send_rows.shape
    halo_rows = partners * length
    columns = blocks + halo_rows // size
    local, far = steps = plan(partners, devices // 2)
    count = 1 + len(far)
    state_half = ((local_rows, half), F32)
    list_half = ((halo_rows, half), F32)
    pieces_out = [((len(lists) * length, half), F32) for lists in (local, *(step[2] for step in far))]
    halo_scratch = pltpu.VMEM((2, halo_rows, panels), BF16)
    lists_scratch = pltpu.VMEM((2, halo_rows, half), F32)

    def halves(x, cost):
        return call(halves_kernel, [state_half] * 2, [VMEM], (x,), cost=cost)

    def merge(tiles, cols):
        return call(merge_kernel, [((blocks, columns, size, size), F32)], [SMEM, VMEM], (cols, tiles))[0]

    def split(total, onehot):
        return call(
            split_kernel,
            [((local_rows, 2 * local_rows), BF16), ((local_rows, 2 * halo_rows), BF16), ((halo_rows, 2 * halo_rows), BF16)],
            [VMEM] * 2,
            (total, onehot),
        )

    def exchange(pieces):
        arrived = [pieces[0]]
        for (hop, forward, _, _), piece in zip(far, pieces[1:]):
            pairs = [(d, (d + 2 * hop_of(hop, forward, d // 2)) % devices) for d in range(devices)]
            arrived.append(lax.ppermute(piece, "rows", pairs))
        return arrived

    applies = 2 * STEPS
    for number in range(applies):
        if number == 0:
            rows_other = swap(send_rows)
            state, give = halves(tracers_init, COST)
            state_other = swap(give)
            merged_e = merge(explicit_tiles, explicit_cols)
            merged_e_other = swap(merged_e)
            *pieces, onehot, onehot_other = call(
                functools.partial(first_kernel, steps),
                pieces_out + [((halo_rows, local_rows), BF16)] * 2,
                [VMEM] * 4,
                (state, state_other, send_rows, rows_other),
                [lists_scratch],
            )
            states = (state, state_other)
            later_tiles, later_cols = implicit_tiles, implicit_cols
        else:
            pieces = call(
                functools.partial(payload_kernel, steps),
                pieces_out,
                [VMEM] * (4 + count),
                (*picks, matrix[0][2], matrix[1][2], *arrived),
                [halo_scratch, lists_scratch],
            )
        fresh = exchange(pieces)
        if number == 0:
            give_s = halves(source, COST // 100)
            sources = (give_s[0], swap(give_s[1]))
            matrix_e = (split(merged_e, onehot), split(merged_e_other, onehot_other))
            merged_i = merge(later_tiles, later_cols)
            merged_i_other = swap(merged_i)
        if number == 1:
            matrix_i = (split(merged_i, onehot), split(merged_i_other, onehot_other))
        last_matrix = matrix if number else None
        matrix = matrix_i if number % 2 else matrix_e
        has_source = number % 2 == 0
        args = (onehot, onehot_other, matrix[0][0], matrix[1][0])
        if has_source:
            args += sources
        args += tuple(states)
        if number:
            args += (last_matrix[0][1], last_matrix[1][1], *arrived)
        out = call(
            functools.partial(own_kernel, steps, has_source, number == 0, number == applies - 1),
            [state_half] * 2 + [list_half] * (2 if number < applies - 1 else 0),
            [VMEM] * len(args),
            args,
            [halo_scratch] if number else [],
        )
        states, picks = out[:2], out[2:]
        arrived = fresh

    whole = [((local_rows, panels), F32)]
    done = pltpu.SemaphoreType.DMA
    got = swap(
        call(
            functools.partial(give_back_kernel, steps),
            [state_half],
            [VMEM] * (2 + count),
            (states[1], matrix[1][1], *arrived),
            [halo_scratch],
        )[0]
    )
    begun = call(
        functools.partial(keep_kernel, steps),
        whole,
        [VMEM] * (2 + count),
        (states[0], matrix[0][1], *arrived),
        [pltpu.VMEM((local_rows, half), F32), done, halo_scratch],
        out_specs=[ANY],
    )
    return call(join_kernel, whole, [VMEM, ANY], (got, *begun), [done], out_specs=[ANY], aliases={1: 0})[0]


def solution(mesh):
    return jax.shard_map(
        on_device,
        mesh=mesh,
        in_specs=(
            P("rows", None),
            P("rows", None),
            P("rows", None, None, None),
            P("rows", None, None, None),
            P("rows", None),
            P("rows", None),
            P("rows", None),
        ),
        out_specs=P("rows", None),
        check_vma=False,
    )
```

```python
import functools

import jax
import jax.numpy as jnp
from jax import lax
from jax.experimental import pallas as pl
from jax.experimental.pallas import tpu as pltpu
from jax.sharding import PartitionSpec as P


STEPS = 3
GRANT = 14 * 2**20
COST = 10**9

VMEM = pl.BlockSpec(memory_space=pltpu.VMEM)
ANY = pl.BlockSpec(memory_space=pl.ANY)
F32, BF16 = jnp.float32, jnp.bfloat16


def call(kernel, outs, in_specs, args, scratch=(), grant=GRANT, out_specs=None, aliases=None, cost=COST):
    return pl.pallas_call(
        kernel,
        out_shape=[jax.ShapeDtypeStruct(shape, dtype) for shape, dtype in outs],
        in_specs=in_specs,
        out_specs=out_specs or [VMEM] * len(outs),
        scratch_shapes=list(scratch),
        input_output_aliases=aliases or {},
        cost_estimate=pl.CostEstimate(flops=cost, bytes_accessed=0, transcendentals=0),
        compiler_params=pltpu.CompilerParams(vmem_limit_bytes=grant),
    )(*args)


def partner_offset(offset_index):
    return (offset_index // 2 + 1) * (1 if offset_index % 2 == 0 else -1)


def plan(partners, pairs):
    found = {}
    for sender in range(2):
        for offset_index in range(partners):
            to = sender + partner_offset(offset_index)
            found.setdefault(to // 2, []).append((sender, offset_index, to % 2))
    local = found.pop(0)
    reach = max(found)
    if reach == 2 and pairs % 4 == 0:
        order = ((2, (1, 0, 1, 1)), (1, (0, 1, 0, 1)), (2, (0, 1, 0, 0)), (1, (1, 0, 1, 0)))
    else:
        order = [(hop, (forward,)) for forward in (1, 0) for hop in range(1, reach + 1)]
    return local, [(hop, forward, found[-hop], found[hop]) for hop, forward in order]


def hop_of(hop, forward, pair):
    return hop if forward[pair % len(forward)] else -hop


def by_pair(table, pair):
    if len(set(table)) == 1:
        return table[0]
    if pair is not None:
        return table[pair % len(table)]
    pair = lax.rem(lax.axis_index("rows") // 2, len(table))
    value = table[0]
    for i in range(1, len(table)):
        value = jnp.where(pair == i, table[i], value)
    return value


def sent_forward(step, pair):
    return by_pair(step[1], pair)


def came_forward(step, pair):
    hop, forward = step[:2]
    count = len(forward)
    table = [0] * count
    for sender in range(count):
        table[(sender + hop_of(hop, forward, sender)) % count] = forward[sender]
    return by_pair(table, pair)


def on_each_pair(steps, body):
    count = max(len(step[1]) for step in steps[1])
    for pair in range(count):

        @pl.when(lax.rem(lax.axis_index("rows") // 2, count) == pair)
        def _(pair=pair):
            body(pair)


def blend(backward, forward, is_forward):
    return backward if backward == forward else backward + is_forward * (forward - backward)


def block(index, length):
    if isinstance(index, int):
        return slice(index * length, (index + 1) * length)
    return pl.ds(pl.multiple_of(index * length, 16), length)


def role_slot(role):
    return side() if role == 0 else 1 - side()


def side():
    return lax.rem(lax.axis_index("rows"), 2)


def swap(x):
    devices = lax.axis_size("rows")
    return lax.ppermute(x, "rows", [(i, i ^ 1) for i in range(devices)])


def split2(x):
    high = x.astype(BF16)
    return high, (x - high.astype(F32)).astype(BF16)


def dot(a, b):
    return jnp.dot(a, b, preferred_element_type=F32)


def product(m, x):
    half = x.shape[1] // 2
    got = dot(m, jnp.concatenate([x, x], axis=0))
    return got[:, :half] + got[:, half:]


def terms(x):
    return jnp.concatenate(split2(x), axis=1)


def pick_rows(onehot, x):
    half = x.shape[1]
    got = dot(onehot, terms(x))
    return got[:, :half] + got[:, half:]


def on_each_side(body):
    for place in range(2):

        @pl.when(side() == place)
        def _(place=place):
            body(place)


def fill_onehot(rows, onehot):
    lists, length = rows.shape
    width = onehot.shape[1]
    down = lax.broadcasted_iota(jnp.int32, (length, length), 0)
    along = lax.broadcasted_iota(jnp.int32, (length, length), 1)
    lanes = lax.broadcasted_iota(jnp.int32, (length, width), 1)
    for i in range(lists):
        spread = jnp.broadcast_to(rows[i : i + 1, :], (length, length))
        column = jnp.sum(jnp.where(down == along, spread, 0).astype(F32), axis=1, keepdims=True)
        hit = jnp.broadcast_to(column, (length, width)) == lanes.astype(F32)
        onehot[i * length : (i + 1) * length, :] = jnp.where(hit, 1.0, 0.0).astype(BF16)


def halves_kernel(x, keep, give):
    half = keep.shape[1]

    def body(place):
        keep[...] = x[:, place * half : (place + 1) * half]
        give[...] = x[:, (1 - place) * half : (2 - place) * half]

    on_each_side(body)


def merge_kernel(columns_in, tiles, total, columns, done):
    fetch = pltpu.make_async_copy(columns_in, columns, done)
    fetch.start()
    total[...] = jnp.zeros_like(total)
    fetch.wait()
    for block in range(tiles.shape[0]):
        for slot in range(tiles.shape[1]):
            column = columns[block, slot]
            total[block, column] += tiles[block, slot]


def split_kernel(total, onehot, own, far, out):
    blocks, columns, size, _ = total.shape

    def put(to, first, last):
        for block in range(blocks):
            at = slice(block * size, (block + 1) * size)
            for column in range(first, last):
                place = (column - first) * size
                low_place = place + to.shape[1] // 2
                to[at, place : place + size], to[at, low_place : low_place + size] = split2(total[block, column])

    put(far, blocks, columns)
    out[...] = dot(onehot[...], far[...]).astype(BF16)
    put(own, 0, blocks)


def deal(steps, lists, outs, pair=None):
    local, far = steps
    length = outs[0].shape[0] // len(local)
    for i, (sender, index, _) in enumerate(local):
        outs[0][block(i, length), :] = lists[sender, block(index, length), :]
    for step, out in zip(far, outs[1:]):
        is_forward = sent_forward(step, pair)
        for i, (backward, forward) in enumerate(zip(*step[2:])):
            sender = blend(backward[0], forward[0], is_forward)
            index = blend(backward[1], forward[1], is_forward)
            out[block(i, length), :] = lists[sender, block(index, length), :]


def collect(steps, arrived, halo, pair=None):
    local, far = steps
    length = arrived[0].shape[0] // len(local)
    for i, (_, index, receiver) in enumerate(local):
        halo[receiver, block(index, length), :] = terms(arrived[0][block(i, length), :])
    for step, piece in zip(far, arrived[1:]):
        is_forward = came_forward(step, pair)
        for i, (backward, forward) in enumerate(zip(*step[2:])):
            receiver = blend(backward[2], forward[2], is_forward)
            index = blend(backward[1], forward[1], is_forward)
            halo[receiver, block(index, length), :] = terms(piece[block(i, length), :])


def first_kernel(steps, mine, other, rows_mine, rows_other, *refs):
    *outs, onehot_mine, onehot_other, lists = refs
    for role, (rows, onehot, state) in enumerate(
        ((rows_mine, onehot_mine, mine), (rows_other, onehot_other, other))
    ):
        fill_onehot(rows, onehot)
        lists[role_slot(role)] = pick_rows(onehot[...], state[...])
    on_each_pair(steps, lambda pair: deal(steps, lists, outs, pair))


def own_kernel(steps, has_source, first, last, *refs):
    refs = list(refs)

    def take(count):
        taken = refs[:count]
        del refs[:count]
        return taken

    onehots, owns = take(2), take(2)
    sources = take(2) if has_source else None
    states = take(2)
    if not first:
        fars, arrived = take(2), take(1 + len(steps[1]))
    bases = take(2)
    picks = None if last else take(2)
    now = [state[...] for state in states]
    if not first:
        (halo,) = refs
        collect(steps, arrived, halo)
        now = [now[role] + product(fars[role][...], halo[role_slot(role)]) for role in range(2)]
    total = [now[role] + product(owns[role][...], terms(now[role])) for role in range(2)]
    if has_source:
        total = [total[role] + sources[role][...] for role in range(2)]
    for role in range(2):
        bases[role][...] = total[role]
        if not last:
            picks[role][...] = pick_rows(onehots[role][...], total[role])


def payload_kernel(steps, *refs):
    count = 1 + len(steps[1])
    picks, outs_of = refs[:2], refs[2:4]
    arrived, outs = refs[4 : 4 + count], refs[4 + count : 4 + 2 * count]
    halo, lists = refs[4 + 2 * count :]

    def body(place, pair):
        collect(steps, arrived, halo, pair)
        for role in range(2):
            slot = role ^ place
            lists[slot] = picks[role][...] + product(outs_of[role][...], halo[slot])
        deal(steps, lists, outs, pair)

    on_each_pair(steps, lambda pair: on_each_side(lambda place: body(place, pair)))


def give_back_kernel(steps, base, far, *refs):
    *arrived, out, halo = refs
    collect(steps, arrived, halo)
    out[...] = base[...] + product(far[...], halo[role_slot(1)])


def store_half(half, out, place, done):
    width = half.shape[1]
    copy = pltpu.make_async_copy(half, out.at[:, place * width : (place + 1) * width], done)
    copy.start()
    copy.wait()


def keep_kernel(steps, base, far, *refs):
    *arrived, out, half, done, halo = refs
    collect(steps, arrived, halo)
    half[...] = base[...] + product(far[...], halo[role_slot(0)])
    on_each_side(lambda place: store_half(half, out, place, done))


def join_kernel(got, begun, out, done):
    on_each_side(lambda place: store_half(got, out, 1 - place, done))


def on_device(
    tracers_init, source, explicit_tiles, implicit_tiles, explicit_cols, implicit_cols, send_rows
):
    devices = lax.axis_size("rows")
    local_rows, panels = tracers_init.shape
    half = panels // 2
    blocks, slots, size, _ = explicit_tiles.shape
    partners, length = send_rows.shape
    halo_rows = partners * length
    columns = blocks + halo_rows // size
    local, far = steps = plan(partners, devices // 2)
    count = 1 + len(far)
    state_half = ((local_rows, half), F32)
    list_half = ((halo_rows, half), F32)
    pieces_out = [((len(lists) * length, half), F32) for lists in (local, *(step[2] for step in far))]
    halo_scratch = pltpu.VMEM((2, halo_rows, panels), BF16)
    lists_scratch = pltpu.VMEM((2, halo_rows, half), F32)

    def halves(x, cost):
        return call(halves_kernel, [state_half] * 2, [VMEM], (x,), cost=cost)

    def merge(tiles, cols):
        return call(
            merge_kernel,
            [((blocks, columns, size, size), F32)],
            [ANY, VMEM],
            (cols, tiles),
            [pltpu.SMEM((blocks, slots), jnp.int32), pltpu.SemaphoreType.DMA],
        )[0]

    def split(total, onehot):
        return call(
            split_kernel,
            [((local_rows, 2 * local_rows), BF16), ((local_rows, 2 * halo_rows), BF16), ((halo_rows, 2 * halo_rows), BF16)],
            [VMEM] * 2,
            (total, onehot),
        )

    def exchange(pieces):
        arrived = [pieces[0]]
        for (hop, forward, _, _), piece in zip(far, pieces[1:]):
            pairs = [(d, (d + 2 * hop_of(hop, forward, d // 2)) % devices) for d in range(devices)]
            arrived.append(lax.ppermute(piece, "rows", pairs))
        return arrived

    applies = 2 * STEPS
    for number in range(applies):
        if number == 0:
            rows_other = swap(send_rows)
            state, give = halves(tracers_init, COST)
            state_other = swap(give)
            merged_e = merge(explicit_tiles, explicit_cols)
            merged_e_other = swap(merged_e)
            *pieces, onehot, onehot_other = call(
                functools.partial(first_kernel, steps),
                pieces_out + [((halo_rows, local_rows), BF16)] * 2,
                [VMEM] * 4,
                (state, state_other, send_rows, rows_other),
                [lists_scratch],
            )
            states = (state, state_other)
            later_tiles, later_cols = implicit_tiles, implicit_cols
        else:
            pieces = call(
                functools.partial(payload_kernel, steps),
                pieces_out,
                [VMEM] * (4 + count),
                (*picks, matrix[0][2], matrix[1][2], *arrived),
                [halo_scratch, lists_scratch],
            )
        fresh = exchange(pieces)
        if number == 0:
            give_s = halves(source, COST // 100)
            sources = (give_s[0], swap(give_s[1]))
            matrix_e = (split(merged_e, onehot), split(merged_e_other, onehot_other))
            merged_i = merge(later_tiles, later_cols)
            merged_i_other = swap(merged_i)
        if number == 1:
            matrix_i = (split(merged_i, onehot), split(merged_i_other, onehot_other))
        last_matrix = matrix if number else None
        matrix = matrix_i if number % 2 else matrix_e
        has_source = number % 2 == 0
        args = (onehot, onehot_other, matrix[0][0], matrix[1][0])
        if has_source:
            args += sources
        args += tuple(states)
        if number:
            args += (last_matrix[0][1], last_matrix[1][1], *arrived)
        out = call(
            functools.partial(own_kernel, steps, has_source, number == 0, number == applies - 1),
            [state_half] * 2 + [list_half] * (2 if number < applies - 1 else 0),
            [VMEM] * len(args),
            args,
            [halo_scratch] if number else [],
        )
        states, picks = out[:2], out[2:]
        arrived = fresh

    whole = [((local_rows, panels), F32)]
    done = pltpu.SemaphoreType.DMA
    got = swap(
        call(
            functools.partial(give_back_kernel, steps),
            [state_half],
            [VMEM] * (2 + count),
            (states[1], matrix[1][1], *arrived),
            [halo_scratch],
        )[0]
    )
    begun = call(
        functools.partial(keep_kernel, steps),
        whole,
        [VMEM] * (2 + count),
        (states[0], matrix[0][1], *arrived),
        [pltpu.VMEM((local_rows, half), F32), done, halo_scratch],
        out_specs=[ANY],
    )
    return call(join_kernel, whole, [VMEM, ANY], (got, *begun), [done], out_specs=[ANY], aliases={1: 0})[0]


def solution(mesh):
    return jax.shard_map(
        on_device,
        mesh=mesh,
        in_specs=(
            P("rows", None),
            P("rows", None),
            P("rows", None, None, None),
            P("rows", None, None, None),
            P("rows", None),
            P("rows", None),
            P("rows", None),
        ),
        out_specs=P("rows", None),
        check_vma=False,
    )
```
